32 devices in a mesh: atoms: 8 (over z, y), chan: 4 (over x, core).
Axes of the slice: x: 2, y: 2, z: 4, core: 2. Of those that a mesh axis runs over, the one named last changes fastest.
Arguments:
- node_x: bfloat16 [49, 128, 512], P(None, 'chan', 'atoms'), may hold values from -6 to 6
- cotangent: bfloat16 [49, 128, 512], P(None, 'chan', 'atoms'), may hold values from -6 to 6
- rotation: bfloat16 [235, 4096], P(None, 'atoms'), may hold values from -2.5 to 2.5
- envelope: float32 [4096], P('atoms'), may hold values from 0.2 to 1
- source: int32 [4096], P('atoms'), may hold values from 0 to 127, as said below
- target: int32 [4096], P('atoms'), may hold values from 0 to 63
- edge_count: int32 [8], P('atoms'), may hold values from 128 to 512, as said below
- send_index: int32 [8, 8, 8], P('atoms'), may hold values from 0 to 63
- halo_count: int32 [8, 8], P(None, 'atoms'), may hold values from 0 to 8, as said below
- weight_zero: bfloat16 [7, 128, 7, 128], P(None, 'chan'), may hold values from -0.1875 to 0.1875
- weight_one: bfloat16 [2, 6, 128, 6, 128], P(None, None, 'chan'), may hold values from -0.15625 to 0.15625
- weight_two: bfloat16 [2, 5, 128, 5, 128], P(None, None, 'chan'), may hold values from -0.15625 to 0.15625
Outputs:
- grad_x: float32 [49, 128, 512], P(None, 'chan', 'atoms')
- grad_weight_zero: float32 [7, 128, 7, 128], P(None, 'chan', None, 'atoms')
- grad_weight_one: float32 [2, 6, 128, 6, 128], P(None, None, 'chan', None, 'atoms')
- grad_weight_two: float32 [2, 5, 128, 5, 128], P(None, None, 'chan', None, 'atoms')
The draws below stay inside these ranges and needn't reach their ends.
Inputs may be any that keep to these rules, and one draw needn't show every extreme that they name: `edge_count`: at least 128 slots of each partition are live, and some partition has all 512 slots live in every draw; live slots come first. `halo_count`: A partition sends nothing to itself and between 4 and 8 atoms to every other partition; partitions whose indices differ by one, cyclically, exchange exactly 8. `source`: A value of 64 or more names slot j of sender p with p other than the edge's own partition and j below halo_count[p, own partition].
All inputs are finite; a program needn't handle non-finite values.
Results may differ from the reference program's by a relative error of at most 0.005.
Values may be sent and summed in bfloat16 or wider, within the bound.
A program may use at most 128 MiB of HBM per device.

```python
import math
import jax
import jax.numpy as jnp
from jax import lax

C = 128
ATOM_DEV = 64
HALO = 8
EDGE_DEV = 512
SECTIONS = 8
ATOMS = 512
EDGES = 4096


def draw_edge_count(key, part):
    first_key, second_key = jax.random.split(key)
    counts = jax.random.randint(first_key, (SECTIONS,), EDGE_DEV // 4, EDGE_DEV + 1)
    fullest = jax.random.randint(second_key, (), 0, SECTIONS)
    return jnp.where(jnp.arange(SECTIONS) == fullest, EDGE_DEV, counts).astype(jnp.int32)


def halo_table(key):
    table_key = jax.random.fold_in(key, 7)
    drawn = jax.random.randint(table_key, (SECTIONS, SECTIONS), HALO // 2, HALO + 1)
    rows = jnp.arange(SECTIONS, dtype=jnp.int32)[:, None]
    cols = jnp.arange(SECTIONS, dtype=jnp.int32)[None, :]
    spread = jnp.abs(rows - cols)
    apart = jnp.minimum(spread, SECTIONS - spread)
    table = jnp.where(apart == 1, HALO, drawn)
    table = jnp.where(apart == 0, 0, table)
    return table.astype(jnp.int32)


def draw_halo_count(key, part):
    return halo_table(key)


def draw_source(key, part):
    table = halo_table(key)
    base_key = jax.random.fold_in(key, 11)
    flag_key, own_key, offset_key, slot_key = jax.random.split(base_key, 4)
    own_flag = jax.random.randint(flag_key, (EDGES,), 0, 5) == 0
    own = jax.random.randint(own_key, (EDGES,), 0, ATOM_DEV)
    home = jnp.arange(EDGES, dtype=jnp.int32) // EDGE_DEV
    offset = jax.random.randint(offset_key, (EDGES,), 1, SECTIONS)
    sender = (home + offset) % SECTIONS
    slot = jax.random.randint(slot_key, (EDGES,), 0, HALO) % table[sender, home]
    halo_value = ATOM_DEV + sender * HALO + slot
    value = jnp.where(own_flag, own, halo_value)
    position = jnp.arange(EDGES, dtype=jnp.int32)
    value = jnp.where(position == 0, 0, value)
    value = jnp.where(position == 1, ATOM_DEV + SECTIONS * HALO - 1, value)
    return value.astype(jnp.int32)


def with_ends(entries, key, smallest, largest):
    index_at = [jax.random.randint(jax.random.fold_in(key, axis), (), 0, length) for axis, length in enumerate(entries.shape)]
    longest = entries.shape.index(max(entries.shape))
    neighbour = index_at[:longest] + [(index_at[longest] + 1) % entries.shape[longest]] + index_at[longest + 1:]
    return entries.at[tuple(index_at)].set(smallest).at[tuple(neighbour)].set(largest)


def levels(key, shape, cuts, least, largest):
    def one(dim, blocks):
        steps = jax.random.uniform(jax.random.fold_in(jax.random.fold_in(key, 6), dim), (blocks,), jnp.float32, least / len(cuts), largest / len(cuts))
        return jnp.repeat(jnp.exp(steps), shape[dim] // blocks).reshape((-1,) + (1,) * (len(shape) - dim - 1))

    gain = one(*cuts[0])
    for cut in cuts[1:]:
        gain = gain * one(*cut)
    return gain


def centred(key, shape, scale, bound, cuts=(), kind=jnp.bfloat16):
    gain = levels(key, shape, cuts, -0.22, 0.18) if cuts else 1.0
    entries = jax.random.normal(key, shape, jnp.float32) * scale * gain
    return jnp.minimum(jnp.maximum(entries, -bound), bound).astype(kind)


def setup_inputs(seed: int = 0) -> dict:
    streams_of = jax.random.split(jax.random.key(seed), 13)
    return {
        "node_x": centred(streams_of[0], (49, C, ATOMS), 1.0, 6.0, ((1, 4), (2, 8))),
        "cotangent": centred(streams_of[1], (49, C, ATOMS), 1.0, 6.0, ((1, 4), (2, 8))),
        "rotation": centred(streams_of[2], (235, EDGES), 0.4, 2.5, ((1, 8),)),
        "envelope": jnp.clip(0.2 + 0.8 * jax.random.uniform(streams_of[3], (EDGES,), jnp.float32) ** levels(streams_of[3], (EDGES,), ((0, 8),), -0.2, 0.2), 0.2, 1.0),
        "source": draw_source(jax.random.fold_in(streams_of[12], 71), 0),
        "target": with_ends(jax.random.randint(streams_of[5], (EDGES,), 0, ATOM_DEV), jax.random.fold_in(streams_of[5], 1), 0, ATOM_DEV - 1).astype(jnp.int32),
        "edge_count": draw_edge_count(jax.random.fold_in(streams_of[12], 71), 0),
        "send_index": with_ends(jax.random.randint(streams_of[7], (SECTIONS, SECTIONS, HALO), 0, ATOM_DEV), jax.random.fold_in(streams_of[7], 1), 0, ATOM_DEV - 1).astype(jnp.int32),
        "halo_count": draw_halo_count(jax.random.fold_in(streams_of[12], 71), 0),
        "weight_zero": centred(streams_of[9], (7, C, 7, C), (7 * C) ** -0.5, 0.1875, ((1, 4),)),
        "weight_one": centred(streams_of[10], (2, 6, C, 6, C), (12 * C) ** -0.5, 0.15625, ((2, 4),)),
        "weight_two": centred(streams_of[11], (2, 5, C, 5, C), (10 * C) ** -0.5, 0.15625, ((2, 4),)),
    }


def frame_pairs():
    listing = [(degree, 0) for degree in range(7)]
    for order in (1, 2):
        listing = listing + [(degree, order) for degree in range(order, 7)]
        listing = listing + [(degree, -order) for degree in range(order, 7)]
    return listing

def rotate_in(packed, feature):
    pieces = []
    offset = 0
    for degree in range(7):
        reach = min(degree, 2)
        height = 2 * reach + 1
        breadth = 2 * degree + 1
        matrix = packed[offset:offset + height * breadth].reshape(height, breadth, packed.shape[1])
        offset = offset + height * breadth
        part_in = feature[degree * degree:degree * degree + breadth]
        pieces.append(jnp.einsum('rke,kce->rce', matrix, part_in))
    return jnp.stack([pieces[degree][min(degree, 2) + order] for degree, order in frame_pairs()])

def rotate_out(packed, framed):
    places = {pair: index for index, pair in enumerate(frame_pairs())}
    pieces = []
    offset = 0
    for degree in range(7):
        reach = min(degree, 2)
        height = 2 * reach + 1
        breadth = 2 * degree + 1
        matrix = packed[offset:offset + height * breadth].reshape(height, breadth, packed.shape[1])
        offset = offset + height * breadth
        stacked = jnp.stack([framed[places[degree, order]] for order in range(-reach, reach + 1)])
        pieces.append(jnp.einsum('rke,rce->kce', matrix, stacked))
    return jnp.concatenate(pieces, axis=0)

def contract(weight, grads):
    first, inner, second, other = weight.shape
    count = grads.shape[2]
    product = jnp.dot(weight.reshape(first * inner, second * other), grads.reshape(second * other, count), preferred_element_type=jnp.float32)
    return product.reshape(first, inner, count)

def outer_sum(rotated, grads):
    first, inner, count = rotated.shape
    second, other = (grads.shape[0], grads.shape[1])
    product = lax.dot_general(rotated.reshape(first * inner, count), grads.reshape(second * other, count), (((1,), (1,)), ((), ())), preferred_element_type=jnp.float32)
    return product.reshape(first, inner, second, other)

def frame_backward(rotated, edge_grad, weight_zero, weight_one, weight_two):
    spans = ((0, 7), (7, 13), (13, 19), (19, 24), (24, 29))
    hpart = [rotated[start:stop] for start, stop in spans]
    gpart = [edge_grad[start:stop] for start, stop in spans]
    backs = [contract(weight_zero, gpart[0])]
    grad_zero = outer_sum(hpart[0], gpart[0])
    grads = []
    for weight, plus, minus in ((weight_one, 1, 2), (weight_two, 3, 4)):
        real_part = weight[0]
        imag_part = weight[1]
        backs.append(contract(real_part, gpart[plus]) + contract(imag_part, gpart[minus]))
        backs.append(contract(real_part, gpart[minus]) - contract(imag_part, gpart[plus]))
        grad_real = outer_sum(hpart[plus], gpart[plus]) + outer_sum(hpart[minus], gpart[minus])
        grad_imag = outer_sum(hpart[plus], gpart[minus]) - outer_sum(hpart[minus], gpart[plus])
        grads.append(jnp.stack([grad_real, grad_imag]))
    return (jnp.concatenate(backs, axis=0), grad_zero, grads[0], grads[1])

def reference(node_x, cotangent, rotation, envelope, source, target, edge_count, send_index, halo_count, weight_zero, weight_one, weight_two):
    channels = node_x.shape[1]
    grad_init = jnp.zeros((49, channels, ATOMS), jnp.float32)
    zero_init = jnp.zeros(weight_zero.shape, jnp.float32)
    one_init = jnp.zeros(weight_one.shape, jnp.float32)
    two_init = jnp.zeros(weight_two.shape, jnp.float32)

    def step(carry, partition):
        grad_all, grad_zero, grad_one, grad_two = carry
        first_slot = partition * EDGE_DEV
        source_ids = lax.dynamic_slice_in_dim(source, first_slot, EDGE_DEV)
        target_ids = lax.dynamic_slice_in_dim(target, first_slot, EDGE_DEV)
        packed = lax.dynamic_slice_in_dim(rotation, first_slot, EDGE_DEV, 1).astype(jnp.float32)
        radial = lax.dynamic_slice_in_dim(envelope, first_slot, EDGE_DEV)
        halo_slot = jnp.maximum(source_ids - ATOM_DEV, 0)
        sender = (halo_slot // HALO).astype(jnp.int32)
        within = (halo_slot % HALO).astype(jnp.int32)
        remote = send_index[sender, partition, within] + sender * ATOM_DEV
        source_atom = jnp.where(source_ids < ATOM_DEV, partition * ATOM_DEV + source_ids, remote).astype(jnp.int32)
        target_atom = (partition * ATOM_DEV + target_ids).astype(jnp.int32)
        usable = (source_ids < ATOM_DEV) | (within < halo_count[sender, partition])
        live = ((jnp.arange(EDGE_DEV, dtype=jnp.int32) < edge_count[partition]) & usable).astype(jnp.float32)
        rotated = rotate_in(packed, node_x[:, :, source_atom].astype(jnp.float32)).astype(jnp.bfloat16)
        edge_grad = (rotate_in(packed, cotangent[:, :, target_atom].astype(jnp.float32)) * (radial * live)).astype(jnp.bfloat16)
        frame_back, add_zero, add_one, add_two = frame_backward(rotated, edge_grad, weight_zero, weight_one, weight_two)
        grad_all = grad_all.at[:, :, source_atom].add(rotate_out(packed, frame_back))
        return ((grad_all, grad_zero + add_zero, grad_one + add_one, grad_two + add_two), None)
    final, unused = lax.scan(step, (grad_init, zero_init, one_init, two_init), jnp.arange(SECTIONS, dtype=jnp.int32))
    factor = 1.0 / math.sqrt(EDGES)
    return (final[0], final[1] * factor, final[2] * factor, final[3] * factor)
```

```python
import functools
import math

import jax
import jax.numpy as jnp
from jax import lax
from jax.experimental import pallas as pl
from jax.experimental.pallas import tpu as pltpu
from jax.sharding import PartitionSpec as P

LANES = 128
BF = jnp.bfloat16
F32 = jnp.float32
VMEM_LIMIT = 56 * 1024 * 1024


def dot(a, b, dims):
    return lax.dot_general(a, b, (dims, ((), ())), preferred_element_type=F32)


NN = ((1,), (0,))
NT = ((1,), (1,))
TN = ((0,), (0,))


def degrees():
    offset = 0
    for degree in range(7):
        reach = min(degree, 2)
        yield degree, reach, offset
        offset += (2 * reach + 1) * (2 * degree + 1)


def cols(block, base=0):
    return pl.ds(pl.multiple_of(base + block * LANES, LANES), LANES)


def rotate_in(rot, raw, block, width, put):
    e = cols(block)
    for degree, reach, offset in degrees():
        breadth = 2 * degree + 1
        acc = [None] * (2 * reach + 1)
        for k in range(breadth):
            v = raw[pl.ds((degree * degree + k) * width, width), e]
            for r in range(2 * reach + 1):
                term = rot[pl.ds(offset + r * breadth + k, 1), e] * v
                acc[r] = term if acc[r] is None else acc[r] + term
        for r in range(2 * reach + 1):
            put(degree, r - reach, acc[r])


def rotate_out(rot, framed, block, width, out):
    e = cols(block)
    spots = {}
    for i, pair in enumerate(frame_pairs()):
        spots[pair] = i
    for degree, reach, offset in degrees():
        breadth = 2 * degree + 1
        u = [
            framed[pl.ds(spots[degree, m] * width, width), e]
            for m in range(-reach, reach + 1)
        ]
        for k in range(breadth):
            acc = None
            for r in range(2 * reach + 1):
                term = rot[pl.ds(offset + r * breadth + k, 1), e] * u[r]
                acc = term if acc is None else acc + term
            out[pl.ds((degree * degree + k) * width, width), e] = acc.astype(BF)


def frame_pairs():
    listing = [(degree, 0) for degree in range(7)]
    for order in (1, 2):
        listing = listing + [(degree, order) for degree in range(order, 7)]
        listing = listing + [(degree, -order) for degree in range(order, 7)]
    return listing


def onehot(ids, rows):
    return (lax.broadcasted_iota(jnp.int32, (rows, ids.shape[1]), 0) == ids).astype(BF)


def onehot_cols(ids, columns):
    return (lax.broadcasted_iota(jnp.int32, (ids.shape[0], columns), 1) == ids).astype(BF)


def prep_kernel(sends, node, cot, send_out, cot_out):
    atoms = node.shape[1]
    send_out[...] = dot(onehot_cols(sends[...], atoms), node[...], NT).astype(BF)
    eye = onehot_cols(lax.broadcasted_iota(jnp.int32, (atoms, 1), 0), atoms)
    cot_out[...] = dot(eye, cot[...], NT).astype(BF)


def frame_kernel(
    exact,
    node,
    recv,
    cot,
    rotation,
    envelope,
    source,
    target,
    count,
    valid,
    gz,
    g1,
    g2,
    *rest,
):
    if exact:
        dz_out, d1_out, d2_out, rot, raw, radial, hz, h1, h2 = rest
    else:
        d_out, rot, raw, radial, hz, h1, h2 = rest
    atoms = node.shape[1]
    slots = recv.shape[0]
    edges = rotation.shape[1]
    blocks = edges // LANES
    groups = cot.shape[0]
    width = node.shape[0] // 49
    channels = gz.shape[0] // 7
    g12 = {1: g1, 2: g2}
    h12 = {1: h1, 2: h2}

    rot[...] = rotation[...].astype(F32)
    ids = source[...]
    own = onehot(ids, atoms)
    halo = onehot(ids - atoms, slots)
    usable = jnp.sum(halo.astype(F32) * valid[...], axis=0, keepdims=True)
    usable = jnp.where(ids < atoms, 1.0, usable)
    place = lax.broadcasted_iota(jnp.int32, (1, edges), 1)
    radial[...] = jnp.where(place < count[...], envelope[...] * usable, 0.0)
    to = onehot(target[...], atoms)

    def group(q, carry):
        raw[...] = dot(cot[q], to, TN)

        def one(block, carry):
            e = cols(block)
            scale = radial[:, e]

            def put(degree, m, value):
                value = (value * scale).astype(BF)
                order = abs(m)
                row = pl.ds(
                    pl.multiple_of((degree - order) * channels + q * width, width), width
                )
                if order == 0:
                    gz[row, e] = value
                else:
                    g12[order][row, cols(block, 0 if m > 0 else edges)] = value

            rotate_in(rot, raw, block, width, put)
            return carry

        return lax.fori_loop(0, blocks, one, carry)

    lax.fori_loop(0, groups, group, 0)

    raw[...] = dot(node[...], own, NN) + dot(recv[...], halo, TN)
    hz[...] = jnp.zeros_like(hz)
    h2[...] = jnp.zeros_like(h2)

    def one_h(block, carry):
        e = cols(block)
        later = cols(block, edges)

        def put(degree, m, value):
            value = value.astype(BF)
            order = abs(m)
            first = (degree - order) * width
            second = (7 - order + degree - order) * width
            if order == 0:
                hz[pl.ds(first, width), e] = value
            elif m > 0:
                h12[order][pl.ds(first, width), e] = value
                h12[order][pl.ds(second, width), later] = value
            else:
                h12[order][pl.ds(first, width), later] = value
                h12[order][pl.ds(second, width), e] = -value

        rotate_in(rot, raw, block, width, put)
        return carry

    lax.fori_loop(0, blocks, one_h, 0)

    if exact:
        dz_out[...] = dot(gz[...], hz[...], NT)
        d1_out[...] = dot(g1[...], h1[...], NT)
        d2_out[...] = dot(g2[...], h2[...], NT)
        return
    parts = d_out.shape[0]
    share = channels // parts
    base = 0
    for count_l, g, h in ((7, gz, hz), (6, g1, h1), (5, g2, h2)):
        for degree in range(count_l):
            part = dot(g[pl.ds(degree * channels, channels), :], h[...], NT).astype(BF)
            for tile in range(h.shape[0] // LANES):
                start = base + tile * count_l * share + degree * share
                for p in range(parts):
                    d_out[p, pl.ds(start, share), :] = part[
                        p * share : (p + 1) * share, tile * LANES : (tile + 1) * LANES
                    ]
        base += h.shape[0] // LANES * count_l * share


def back_kernel(gz, g1, g2, wz, w1, w2, rotation, source, own_out, halo_out, rot, fb, y):
    edges = rotation.shape[1]
    blocks = edges // LANES
    atoms = own_out.shape[1]
    slots = halo_out.shape[0]
    width = wz.shape[0] // 7
    rot[...] = rotation[...].astype(F32)
    fb[pl.ds(0, 7 * width), :] = dot(wz[...], gz[...], NN)
    start = 7 * width
    for count_l, w, g in ((6, w1, g1), (5, w2, g2)):
        rows = count_l * width
        real = dot(w[pl.ds(0, rows), :], g[...], NN)
        imag = dot(w[pl.ds(rows, rows), :], g[...], NN)
        fb[pl.ds(start, rows), :] = real[:, :edges] + imag[:, edges:]
        fb[pl.ds(start + rows, rows), :] = real[:, edges:] - imag[:, :edges]
        start += 2 * rows

    def one(block, carry):
        rotate_out(rot, fb, block, width, y)
        return carry

    lax.fori_loop(0, blocks, one, 0)
    ids = source[...]
    own_out[...] = dot(y[...], onehot(ids, atoms), NT)
    halo_out[...] = dot(onehot(ids - atoms, slots), y[...], NT).astype(BF)


def join_kernel(own, back, sends, out):
    out[...] = own[...] + dot(back[...], onehot_cols(sends[...], own.shape[1]), TN)


def call(kernel, outs, scratch=(), flops=10**8):
    return pl.pallas_call(
        kernel,
        out_shape=outs,
        scratch_shapes=list(scratch),
        compiler_params=pltpu.CompilerParams(vmem_limit_bytes=VMEM_LIMIT),
        cost_estimate=pl.CostEstimate(
            flops=flops, bytes_accessed=8 * 10**6, transcendentals=0
        ),
    )


def on_device(
    node_x,
    cotangent,
    rotation,
    envelope,
    source,
    target,
    edge_count,
    send_index,
    halo_count,
    weight_zero,
    weight_one,
    weight_two,
):
    parts = lax.axis_size("atoms")
    groups = lax.axis_size("chan")
    width = node_x.shape[1]
    channels = width * groups
    atoms = node_x.shape[2]
    halo = send_index.shape[2]
    edges = source.shape[0]
    slots = parts * halo
    rows = 49 * width
    share = channels // parts
    exact = share % 16 != 0
    sds = jax.ShapeDtypeStruct

    node = node_x.reshape(rows, atoms)
    cot = cotangent.reshape(rows, atoms)
    sends = send_index.reshape(slots, 1)
    send_rows, cot_rows = call(
        prep_kernel, (sds((slots, rows), BF), sds((atoms, rows), BF))
    )(sends, node, cot)
    recv = lax.all_to_all(send_rows, "atoms", split_axis=0, concat_axis=0, tiled=True)
    cots = lax.all_gather(cot_rows, "chan", axis=0, tiled=False)

    valid = (
        jnp.arange(halo, dtype=jnp.int32)[None, :] < halo_count[:, 0][:, None]
    ).astype(F32).reshape(slots, 1)
    src = source.reshape(1, edges)
    tgt = target.reshape(1, edges)

    g_shapes = (
        sds((7 * channels, edges), BF),
        sds((6 * channels, 2 * edges), BF),
        sds((5 * channels, 2 * edges), BF),
    )
    pad = lambda n: -(-n // LANES) * LANES
    lz, l1, l2 = pad(7 * width), pad(12 * width), pad(10 * width)
    height = (7 * lz + 6 * l1 + 5 * l2) // LANES * share
    if exact:
        d_shapes = (
            sds((7 * channels, lz), F32),
            sds((6 * channels, l1), F32),
            sds((5 * channels, l2), F32),
        )
    else:
        d_shapes = (sds((parts, height, LANES), BF),)
    made = call(
        functools.partial(frame_kernel, exact),
        g_shapes + d_shapes,
        (
            pltpu.VMEM((235, edges), F32),
            pltpu.VMEM((rows, edges), F32),
            pltpu.VMEM((1, edges), F32),
            pltpu.VMEM((lz, edges), BF),
            pltpu.VMEM((l1, 2 * edges), BF),
            pltpu.VMEM((l2, 2 * edges), BF),
        ),
        flops=10**10,
    )(
        node,
        recv,
        cots,
        rotation,
        envelope.reshape(1, edges),
        src,
        tgt,
        edge_count.reshape(1, 1),
        valid,
    )
    gz, g1, g2 = made[:3]
    factor = 1.0 / math.sqrt(edges * parts)

    if not exact:
        pieces = lax.all_to_all(made[3], "atoms", split_axis=0, concat_axis=0, tiled=True)

    own, halo_rows = call(
        back_kernel,
        (sds((rows, atoms), F32), sds((slots, rows), BF)),
        (
            pltpu.VMEM((235, edges), F32),
            pltpu.VMEM((29 * width, edges), F32),
            pltpu.VMEM((rows, edges), BF),
        ),
        flops=10**10,
    )(
        gz,
        g1,
        g2,
        weight_zero.reshape(7 * width, 7 * channels),
        weight_one.reshape(12 * width, 6 * channels),
        weight_two.reshape(10 * width, 5 * channels),
        rotation,
        src,
    )
    back = lax.all_to_all(halo_rows, "atoms", split_axis=0, concat_axis=0, tiled=True)
    grad_x = call(join_kernel, sds((rows, atoms), F32))(own, back, sends)

    if exact:
        dz = made[3][:, : 7 * width].reshape(7, channels, 7, width)
        d1 = made[4].reshape(6, channels, 2, 6, width)
        d2 = made[5][:, : 10 * width].reshape(5, channels, 2, 5, width)
        dz = lax.psum_scatter(dz, "atoms", scatter_dimension=1, tiled=True)
        d1 = lax.psum_scatter(d1, "atoms", scatter_dimension=1, tiled=True)
        d2 = lax.psum_scatter(d2, "atoms", scatter_dimension=1, tiled=True)
    else:
        total = jnp.sum(pieces.astype(F32), axis=0)

        def take(start, count_l, lanes):
            tiles = lanes // LANES
            size = count_l * share
            got = [total[start + t * size : start + (t + 1) * size] for t in range(tiles)]
            return jnp.concatenate(got, axis=1), start + tiles * size

        dz, start = take(0, 7, lz)
        d1, start = take(start, 6, l1)
        d2, start = take(start, 5, l2)
        dz = dz[:, : 7 * width].reshape(7, share, 7, width)
        d1 = d1[:, : 12 * width].reshape(6, share, 2, 6, width)
        d2 = d2[:, : 10 * width].reshape(5, share, 2, 5, width)
    return (
        grad_x.reshape(49, width, atoms),
        dz.transpose(2, 3, 0, 1) * factor,
        d1.transpose(2, 3, 4, 0, 1) * factor,
        d2.transpose(2, 3, 4, 0, 1) * factor,
    )


def solution(mesh):
    in_specs = (
        P(None, "chan", "atoms"),
        P(None, "chan", "atoms"),
        P(None, "atoms"),
        P("atoms"),
        P("atoms"),
        P("atoms"),
        P("atoms"),
        P("atoms", None, None),
        P(None, "atoms"),
        P(None, "chan", None, None),
        P(None, None, "chan", None, None),
        P(None, None, "chan", None, None),
    )
    out_specs = (
        P(None, "chan", "atoms"),
        P(None, "chan", None, "atoms"),
        P(None, None, "chan", None, "atoms"),
        P(None, None, "chan", None, "atoms"),
    )
    return jax.shard_map(
        on_device, mesh=mesh, in_specs=in_specs, out_specs=out_specs, check_vma=False
    )
```

```python
import functools
import math

import jax
import jax.numpy as jnp
from jax import lax
from jax.experimental import pallas as pl
from jax.experimental.pallas import tpu as pltpu
from jax.sharding import PartitionSpec as P

LANES = 128
BF = jnp.bfloat16
F32 = jnp.float32
VMEM_LIMIT = 56 * 1024 * 1024
MESH = pl.DeviceIdType.MESH


def dot(a, b, dims):
    return lax.dot_general(a, b, (dims, ((), ())), preferred_element_type=F32)


NN = ((1,), (0,))
NT = ((1,), (1,))
TN = ((0,), (0,))


def degrees():
    offset = 0
    for degree in range(7):
        reach = min(degree, 2)
        yield degree, reach, offset
        offset += (2 * reach + 1) * (2 * degree + 1)


def cols(block, base=0):
    return pl.ds(pl.multiple_of(base + block * LANES, LANES), LANES)


def rotate_in(rot, raw, block, width, put):
    e = cols(block)
    for degree, reach, offset in degrees():
        breadth = 2 * degree + 1
        acc = [None] * (2 * reach + 1)
        for k in range(breadth):
            v = raw[pl.ds((degree * degree + k) * width, width), e]
            for r in range(2 * reach + 1):
                term = rot[pl.ds(offset + r * breadth + k, 1), e] * v
                acc[r] = term if acc[r] is None else acc[r] + term
        for r in range(2 * reach + 1):
            put(degree, r - reach, acc[r])


def rotate_out(rot, framed, block, width, out):
    e = cols(block)
    spots = {}
    for i, pair in enumerate(frame_pairs()):
        spots[pair] = i
    for degree, reach, offset in degrees():
        breadth = 2 * degree + 1
        u = [
            framed[pl.ds(spots[degree, m] * width, width), e]
            for m in range(-reach, reach + 1)
        ]
        for k in range(breadth):
            acc = None
            for r in range(2 * reach + 1):
                term = rot[pl.ds(offset + r * breadth + k, 1), e] * u[r]
                acc = term if acc is None else acc + term
            out[pl.ds((degree * degree + k) * width, width), e] = acc.astype(BF)


def frame_pairs():
    listing = [(degree, 0) for degree in range(7)]
    for order in (1, 2):
        listing = listing + [(degree, order) for degree in range(order, 7)]
        listing = listing + [(degree, -order) for degree in range(order, 7)]
    return listing


def onehot(ids, rows):
    return (lax.broadcasted_iota(jnp.int32, (rows, ids.shape[1]), 0) == ids).astype(BF)


def onehot_cols(ids, columns):
    return (lax.broadcasted_iota(jnp.int32, (ids.shape[0], columns), 1) == ids).astype(BF)


def prep_kernel(sends, node, cot, send_out, cot_out):
    atoms = node.shape[1]
    send_out[...] = dot(onehot_cols(sends[...], atoms), node[...], NT).astype(BF)
    eye = onehot_cols(lax.broadcasted_iota(jnp.int32, (atoms, 1), 0), atoms)
    cot_out[...] = dot(eye, cot[...], NT).astype(BF)


def frame_kernel(
    exact,
    node,
    recv,
    cot,
    rotation,
    envelope,
    source,
    target,
    count,
    valid,
    gz,
    g1,
    g2,
    *rest,
):
    if exact:
        dz_out, d1_out, d2_out, rot, raw, radial, hz, h1, h2 = rest
    else:
        d_out, rot, raw, radial, hz, h1, h2 = rest
    atoms = node.shape[1]
    slots = recv.shape[0]
    edges = rotation.shape[1]
    blocks = edges // LANES
    groups = cot.shape[0]
    width = node.shape[0] // 49
    channels = gz.shape[0] // 7
    g12 = {1: g1, 2: g2}
    h12 = {1: h1, 2: h2}

    rot[...] = rotation[...].astype(F32)
    ids = source[...]
    own = onehot(ids, atoms)
    halo = onehot(ids - atoms, slots)
    usable = jnp.sum(halo.astype(F32) * valid[...], axis=0, keepdims=True)
    usable = jnp.where(ids < atoms, 1.0, usable)
    place = lax.broadcasted_iota(jnp.int32, (1, edges), 1)
    radial[...] = jnp.where(place < count[...], envelope[...] * usable, 0.0)
    to = onehot(target[...], atoms)

    def group(q, carry):
        raw[...] = dot(cot[q], to, TN)

        def one(block, carry):
            e = cols(block)
            scale = radial[:, e]

            def put(degree, m, value):
                value = (value * scale).astype(BF)
                order = abs(m)
                row = pl.ds(
                    pl.multiple_of((degree - order) * channels + q * width, width), width
                )
                if order == 0:
                    gz[row, e] = value
                else:
                    g12[order][row, cols(block, 0 if m > 0 else edges)] = value

            rotate_in(rot, raw, block, width, put)
            return carry

        return lax.fori_loop(0, blocks, one, carry)

    lax.fori_loop(0, groups, group, 0)

    raw[...] = dot(node[...], own, NN) + dot(recv[...], halo, TN)
    hz[...] = jnp.zeros_like(hz)
    h2[...] = jnp.zeros_like(h2)

    def one_h(block, carry):
        e = cols(block)
        later = cols(block, edges)

        def put(degree, m, value):
            value = value.astype(BF)
            order = abs(m)
            first = (degree - order) * width
            second = (7 - order + degree - order) * width
            if order == 0:
                hz[pl.ds(first, width), e] = value
            elif m > 0:
                h12[order][pl.ds(first, width), e] = value
                h12[order][pl.ds(second, width), later] = value
            else:
                h12[order][pl.ds(first, width), later] = value
                h12[order][pl.ds(second, width), e] = -value

        rotate_in(rot, raw, block, width, put)
        return carry

    lax.fori_loop(0, blocks, one_h, 0)

    if exact:
        dz_out[...] = dot(gz[...], hz[...], NT)
        d1_out[...] = dot(g1[...], h1[...], NT)
        d2_out[...] = dot(g2[...], h2[...], NT)
        return
    parts = d_out.shape[0]
    share = channels // parts
    base = 0
    for count_l, g, h in ((7, gz, hz), (6, g1, h1), (5, g2, h2)):
        for degree in range(count_l):
            part = dot(g[pl.ds(degree * channels, channels), :], h[...], NT).astype(BF)
            for tile in range(h.shape[0] // LANES):
                start = base + tile * count_l * share + degree * share
                for p in range(parts):
                    spot = (p % 2) * (parts // 2) + p // 2
                    d_out[spot, pl.ds(start, share), :] = part[
                        p * share : (p + 1) * share, tile * LANES : (tile + 1) * LANES
                    ]
        base += h.shape[0] // LANES * count_l * share


def back_kernel(gz, g1, g2, wz, w1, w2, rotation, source, own_out, halo_out, rot, fb, y):
    edges = rotation.shape[1]
    blocks = edges // LANES
    atoms = own_out.shape[1]
    slots = halo_out.shape[0]
    width = wz.shape[0] // 7
    rot[...] = rotation[...].astype(F32)
    fb[pl.ds(0, 7 * width), :] = dot(wz[...], gz[...], NN)
    start = 7 * width
    for count_l, w, g in ((6, w1, g1), (5, w2, g2)):
        rows = count_l * width
        real = dot(w[pl.ds(0, rows), :], g[...], NN)
        imag = dot(w[pl.ds(rows, rows), :], g[...], NN)
        fb[pl.ds(start, rows), :] = real[:, :edges] + imag[:, edges:]
        fb[pl.ds(start + rows, rows), :] = real[:, edges:] - imag[:, :edges]
        start += 2 * rows

    def one(block, carry):
        rotate_out(rot, fb, block, width, y)
        return carry

    lax.fori_loop(0, blocks, one, 0)
    ids = source[...]
    own_out[...] = dot(y[...], onehot(ids, atoms), NT)
    halo_out[...] = dot(onehot(ids - atoms, slots), y[...], NT).astype(BF)


def join_kernel(own, back, sends, out):
    out[...] = own[...] + dot(back[...], onehot_cols(sends[...], own.shape[1]), TN)


def exchange_kernel(
    sends,
    node,
    cot,
    recv_out,
    cot_out,
    mine,
    land,
    cots,
    halo_sent,
    halo_got,
    chan_sent,
    chan_got,
):
    parts, halo, _ = land.shape
    groups = cots.shape[0]
    atoms = node.shape[1]
    me = lax.axis_index("atoms")
    group = lax.axis_index("chan")
    barrier = pltpu.get_barrier_semaphore()
    for k in range(1, parts):
        pl.semaphore_signal(
            barrier, inc=1, device_id={"atoms": lax.rem(me + k, parts)}, device_id_type=MESH
        )
    for k in range(1, groups):
        pl.semaphore_signal(
            barrier, inc=1, device_id={"chan": lax.rem(group + k, groups)}, device_id_type=MESH
        )
    eye = onehot_cols(lax.broadcasted_iota(jnp.int32, (atoms, 1), 0), atoms)
    cots[group] = dot(eye, cot[...], NT).astype(BF)
    picked = dot(onehot_cols(sends[...], atoms), node[...], NT).astype(BF)
    for p in range(parts):
        mine[p] = picked[p * halo : (p + 1) * halo, :]
    pl.semaphore_wait(barrier, parts + groups - 2)
    copies = []
    for k in range(1, parts):
        peer = lax.rem(me + k, parts)
        copies.append(
            pltpu.make_async_remote_copy(
                src_ref=mine.at[peer],
                dst_ref=land.at[me],
                send_sem=halo_sent.at[k],
                recv_sem=halo_got.at[k],
                device_id={"atoms": peer},
                device_id_type=MESH,
            )
        )
    for k in range(1, groups):
        peer = lax.rem(group + k, groups)
        copies.append(
            pltpu.make_async_remote_copy(
                src_ref=cots.at[group],
                dst_ref=cots.at[group],
                send_sem=chan_sent.at[k],
                recv_sem=chan_got.at[k],
                device_id={"chan": peer},
                device_id_type=MESH,
            )
        )
    for copy in copies:
        copy.start()
    land[me] = mine[me]
    for copy in copies:
        copy.wait()
    recv_out[...] = land[...]
    cot_out[...] = cots[...]


def finish_kernel(
    factor,
    gz,
    g1,
    g2,
    wz_in,
    w1_in,
    w2_in,
    rotation,
    source,
    sends,
    pieces,
    x_out,
    dz_out,
    d1_out,
    d2_out,
    wz,
    w1,
    w2,
    rot,
    fb,
    y,
    halo_mine,
    halo_land,
    near,
    passing,
    far,
    total,
    near_sent,
    near_got,
    far_sent,
    far_got,
    halo_sent,
    halo_got,
):
    edges = rotation.shape[1]
    blocks = edges // LANES
    atoms = x_out.shape[1]
    parts, halo, rows_x = halo_land.shape
    slots = parts * halo
    width = wz.shape[0] // 7
    channels = wz.shape[1] // 7
    share = channels // parts
    half = parts // 2
    me = lax.axis_index("atoms")
    line, side = me // 2, lax.rem(me, 2)
    other = line * 2 + 1 - side

    barrier = pltpu.get_barrier_semaphore()
    for k in range(1, parts):
        pl.semaphore_signal(
            barrier, inc=1, device_id={"atoms": lax.rem(me + k, parts)}, device_id_type=MESH
        )
    rot[...] = rotation[...].astype(F32)
    for i in range(7):
        for j in range(7):
            wz[i * width : (i + 1) * width, j * channels : (j + 1) * channels] = wz_in[i, j]
    for count_l, w, w_in in ((6, w1, w1_in), (5, w2, w2_in)):
        for part in range(2):
            for i in range(count_l):
                for j in range(count_l):
                    at = (part * count_l + i) * width
                    w[at : at + width, j * channels : (j + 1) * channels] = w_in[part, i, j]
    pl.semaphore_wait(barrier, parts - 1)

    lanes = ((7, dz_out), (6, d1_out), (5, d2_out))
    tiles = [-(-(count_l if i == 0 else 2 * count_l) * width // LANES) for i, (count_l, _) in enumerate(lanes)]
    chunks = []
    start = 0
    for (count_l, _), t in zip(lanes, tiles):
        size = t * count_l * share
        chunks.append((start, size))
        start += size

    near_copies = []
    for c, (start, size) in enumerate(chunks):
        copy = pltpu.make_async_remote_copy(
            src_ref=pieces.at[pl.ds((1 - side) * half, half), pl.ds(start, size), :],
            dst_ref=near.at[:, pl.ds(start, size), :],
            send_sem=near_sent.at[c],
            recv_sem=near_got.at[c],
            device_id={"atoms": other},
            device_id_type=MESH,
        )
        copy.start()
        near_copies.append(copy)

    far_copies = []

    def pass_on(c):
        start, size = chunks[c]
        near_copies[c].wait_recv()
        window = pl.ds(start, size)
        for k in range(half):
            place = lax.rem(line + k, half)
            value = pieces[side * half + place, window, :].astype(F32) + near[
                place, window, :
            ].astype(F32)
            if k == 0:
                total[window, :] = value
                continue
            passing[k - 1, window, :] = value.astype(BF)
            copy = pltpu.make_async_remote_copy(
                src_ref=passing.at[k - 1, window, :],
                dst_ref=far.at[k - 1, window, :],
                send_sem=far_sent.at[c, k - 1],
                recv_sem=far_got.at[c, k - 1],
                device_id={"atoms": place * 2 + side},
                device_id_type=MESH,
            )
            copy.start()
            far_copies.append((c, copy))

    fb[pl.ds(0, 7 * width), :] = dot(wz[...], gz[...], NN)
    start = 7 * width
    for count_l, w, g in ((6, w1, g1), (5, w2, g2)):
        rows = count_l * width
        real = dot(w[pl.ds(0, rows), :], g[...], NN)
        imag = dot(w[pl.ds(rows, rows), :], g[...], NN)
        fb[pl.ds(start, rows), :] = real[:, :edges] + imag[:, edges:]
        fb[pl.ds(start + rows, rows), :] = real[:, edges:] - imag[:, :edges]
        start += 2 * rows

    def one(block, carry):
        rotate_out(rot, fb, block, width, y)
        return carry

    lax.fori_loop(0, blocks, one, 0)
    ids = source[...]
    halo_terms = dot(onehot(ids - atoms, slots), y[...], NT).astype(BF)
    for p in range(parts):
        halo_mine[p] = halo_terms[p * halo : (p + 1) * halo, :]
    halo_copies = []
    for k in range(1, parts):
        peer = lax.rem(me + k, parts)
        copy = pltpu.make_async_remote_copy(
            src_ref=halo_mine.at[peer],
            dst_ref=halo_land.at[me],
            send_sem=halo_sent.at[k],
            recv_sem=halo_got.at[k],
            device_id={"atoms": peer},
            device_id_type=MESH,
        )
        copy.start()
        halo_copies.append(copy)
    halo_land[me] = halo_mine[me]
    pass_on(0)
    x_out[...] = dot(y[...], onehot(ids, atoms), NT)
    pass_on(1)
    for copy in halo_copies:
        copy.wait_recv()
    back = halo_land[...].astype(F32).reshape(slots, rows_x).astype(BF)
    x_out[...] += dot(back, onehot_cols(sends[...], atoms), TN)
    pass_on(2)

    for c, (count_l, out) in enumerate(lanes):
        start, size = chunks[c]
        window = pl.ds(start, size)
        value = total[window, :]
        for at, copy in far_copies:
            if at == c:
                copy.wait_recv()
        for k in range(half - 1):
            value = value + far[k, window, :].astype(F32)
        value = value * factor
        for i in range(count_l if c == 0 else 2 * count_l):
            tile, lane = divmod(i * width, LANES)
            for j in range(count_l):
                row = (tile * count_l + j) * share
                cut = value[row : row + share, lane : lane + width]
                if c == 0:
                    out[i, j] = cut
                else:
                    out[i // count_l, i % count_l, j] = cut

    for copy in near_copies + halo_copies + [copy for _, copy in far_copies]:
        copy.wait_send()


def call(kernel, outs, scratch=(), flops=10**8, collective=None):
    if collective is None:
        params = pltpu.CompilerParams(vmem_limit_bytes=VMEM_LIMIT)
    else:
        params = pltpu.CompilerParams(
            vmem_limit_bytes=VMEM_LIMIT, collective_id=collective, has_side_effects=True
        )
    return pl.pallas_call(
        kernel,
        out_shape=outs,
        scratch_shapes=list(scratch),
        compiler_params=params,
        cost_estimate=pl.CostEstimate(
            flops=flops, bytes_accessed=8 * 10**6, transcendentals=0
        ),
    )


def on_device(
    node_x,
    cotangent,
    rotation,
    envelope,
    source,
    target,
    edge_count,
    send_index,
    halo_count,
    weight_zero,
    weight_one,
    weight_two,
):
    parts = lax.axis_size("atoms")
    groups = lax.axis_size("chan")
    width = node_x.shape[1]
    channels = width * groups
    atoms = node_x.shape[2]
    halo = send_index.shape[2]
    edges = source.shape[0]
    slots = parts * halo
    rows = 49 * width
    share = channels // parts
    exact = parts != 8 or share % 16 != 0
    sds = jax.ShapeDtypeStruct

    node = node_x.reshape(rows, atoms)
    cot = cotangent.reshape(rows, atoms)
    sends = send_index.reshape(slots, 1)
    dma = pltpu.SemaphoreType.DMA
    if exact:
        send_rows, cot_rows = call(
            prep_kernel, (sds((slots, rows), BF), sds((atoms, rows), BF))
        )(sends, node, cot)
        recv = lax.all_to_all(send_rows, "atoms", split_axis=0, concat_axis=0, tiled=True)
        cots = lax.all_gather(cot_rows, "chan", axis=0, tiled=False)
    else:
        recv, cots = call(
            exchange_kernel,
            (sds((parts, halo, rows), BF), sds((groups, atoms, rows), BF)),
            (
                pltpu.VMEM((parts, halo, rows), BF),
                pltpu.VMEM((parts, halo, rows), BF),
                pltpu.VMEM((groups, atoms, rows), BF),
                dma((parts,)),
                dma((parts,)),
                dma((groups,)),
                dma((groups,)),
            ),
            collective=0,
        )(sends, node, cot)
        recv = recv.reshape(slots, rows)

    valid = (
        jnp.arange(halo, dtype=jnp.int32)[None, :] < halo_count[:, 0][:, None]
    ).astype(F32).reshape(slots, 1)
    src = source.reshape(1, edges)
    tgt = target.reshape(1, edges)

    g_shapes = (
        sds((7 * channels, edges), BF),
        sds((6 * channels, 2 * edges), BF),
        sds((5 * channels, 2 * edges), BF),
    )
    pad = lambda n: -(-n // LANES) * LANES
    lz, l1, l2 = pad(7 * width), pad(12 * width), pad(10 * width)
    height = (7 * lz + 6 * l1 + 5 * l2) // LANES * share
    if exact:
        d_shapes = (
            sds((7 * channels, lz), F32),
            sds((6 * channels, l1), F32),
            sds((5 * channels, l2), F32),
        )
    else:
        d_shapes = (sds((parts, height, LANES), BF),)
    made = call(
        functools.partial(frame_kernel, exact),
        g_shapes + d_shapes,
        (
            pltpu.VMEM((235, edges), F32),
            pltpu.VMEM((rows, edges), F32),
            pltpu.VMEM((1, edges), F32),
            pltpu.VMEM((lz, edges), BF),
            pltpu.VMEM((l1, 2 * edges), BF),
            pltpu.VMEM((l2, 2 * edges), BF),
        ),
        flops=10**10,
    )(
        node,
        recv,
        cots,
        rotation,
        envelope.reshape(1, edges),
        src,
        tgt,
        edge_count.reshape(1, 1),
        valid,
    )
    gz, g1, g2 = made[:3]
    factor = 1.0 / math.sqrt(edges * parts)

    if not exact:
        half = parts // 2
        grad_x, dz, d1, d2 = call(
            functools.partial(finish_kernel, factor),
            (
                sds((rows, atoms), F32),
                sds((7, 7, share, width), F32),
                sds((2, 6, 6, share, width), F32),
                sds((2, 5, 5, share, width), F32),
            ),
            (
                pltpu.VMEM((7 * width, 7 * channels), BF),
                pltpu.VMEM((12 * width, 6 * channels), BF),
                pltpu.VMEM((10 * width, 5 * channels), BF),
                pltpu.VMEM((235, edges), F32),
                pltpu.VMEM((29 * width, edges), F32),
                pltpu.VMEM((rows, edges), BF),
                pltpu.VMEM((parts, halo, rows), BF),
                pltpu.VMEM((parts, halo, rows), BF),
                pltpu.VMEM((half, height, LANES), BF),
                pltpu.VMEM((half - 1, height, LANES), BF),
                pltpu.VMEM((half - 1, height, LANES), BF),
                pltpu.VMEM((height, LANES), F32),
                dma((3,)),
                dma((3,)),
                dma((3, half - 1)),
                dma((3, half - 1)),
                dma((parts,)),
                dma((parts,)),
            ),
            flops=10**10,
            collective=1,
        )(
            gz,
            g1,
            g2,
            weight_zero.transpose(0, 2, 1, 3),
            weight_one.transpose(0, 1, 3, 2, 4),
            weight_two.transpose(0, 1, 3, 2, 4),
            rotation,
            src,
            sends,
            made[3],
        )
        return (
            grad_x.reshape(49, width, atoms),
            dz.transpose(0, 3, 1, 2),
            d1.transpose(0, 1, 4, 2, 3),
            d2.transpose(0, 1, 4, 2, 3),
        )

    own, halo_rows = call(
        back_kernel,
        (sds((rows, atoms), F32), sds((slots, rows), BF)),
        (
            pltpu.VMEM((235, edges), F32),
            pltpu.VMEM((29 * width, edges), F32),
            pltpu.VMEM((rows, edges), BF),
        ),
        flops=10**10,
    )(
        gz,
        g1,
        g2,
        weight_zero.reshape(7 * width, 7 * channels),
        weight_one.reshape(12 * width, 6 * channels),
        weight_two.reshape(10 * width, 5 * channels),
        rotation,
        src,
    )
    back = lax.all_to_all(halo_rows, "atoms", split_axis=0, concat_axis=0, tiled=True)
    grad_x = call(join_kernel, sds((rows, atoms), F32))(own, back, sends)

    dz = made[3][:, : 7 * width].reshape(7, channels, 7, width)
    d1 = made[4].reshape(6, channels, 2, 6, width)
    d2 = made[5][:, : 10 * width].reshape(5, channels, 2, 5, width)
    dz = lax.psum_scatter(dz, "atoms", scatter_dimension=1, tiled=True)
    d1 = lax.psum_scatter(d1, "atoms", scatter_dimension=1, tiled=True)
    d2 = lax.psum_scatter(d2, "atoms", scatter_dimension=1, tiled=True)
    return (
        grad_x.reshape(49, width, atoms),
        dz.transpose(2, 3, 0, 1) * factor,
        d1.transpose(2, 3, 4, 0, 1) * factor,
        d2.transpose(2, 3, 4, 0, 1) * factor,
    )


def solution(mesh):
    in_specs = (
        P(None, "chan", "atoms"),
        P(None, "chan", "atoms"),
        P(None, "atoms"),
        P("atoms"),
        P("atoms"),
        P("atoms"),
        P("atoms"),
        P("atoms", None, None),
        P(None, "atoms"),
        P(None, "chan", None, None),
        P(None, None, "chan", None, None),
        P(None, None, "chan", None, None),
    )
    out_specs = (
        P(None, "chan", "atoms"),
        P(None, "chan", None, "atoms"),
        P(None, None, "chan", None, "atoms"),
        P(None, None, "chan", None, "atoms"),
    )
    return jax.shard_map(
        on_device, mesh=mesh, in_specs=in_specs, out_specs=out_specs, check_vma=False
    )
```

```python
import functools
import math

import jax
import jax.numpy as jnp
from jax import lax
from jax.experimental import pallas as pl
from jax.experimental.pallas import tpu as pltpu
from jax.sharding import PartitionSpec as P

LANES = 128
BF = jnp.bfloat16
F32 = jnp.float32
VMEM_LIMIT = 56 * 1024 * 1024
MESH = pl.DeviceIdType.MESH


def dot(a, b, dims):
    return lax.dot_general(a, b, (dims, ((), ())), preferred_element_type=F32)


NN = ((1,), (0,))
NT = ((1,), (1,))
TN = ((0,), (0,))


def degrees():
    offset = 0
    for degree in range(7):
        reach = min(degree, 2)
        yield degree, reach, offset
        offset += (2 * reach + 1) * (2 * degree + 1)


def cols(block, base=0):
    return pl.ds(pl.multiple_of(base + block * LANES, LANES), LANES)


def rotate_in(rot, raw, block, width, put):
    e = cols(block)
    for degree, reach, offset in degrees():
        breadth = 2 * degree + 1
        acc = [None] * (2 * reach + 1)
        for k in range(breadth):
            v = raw[pl.ds((degree * degree + k) * width, width), e]
            for r in range(2 * reach + 1):
                term = rot[pl.ds(offset + r * breadth + k, 1), e] * v
                acc[r] = term if acc[r] is None else acc[r] + term
        for r in range(2 * reach + 1):
            put(degree, r - reach, acc[r])


def rotate_out(rot, framed, block, width, out):
    e = cols(block)
    spots = {}
    for i, pair in enumerate(frame_pairs()):
        spots[pair] = i
    for degree, reach, offset in degrees():
        breadth = 2 * degree + 1
        u = [
            framed[pl.ds(spots[degree, m] * width, width), e]
            for m in range(-reach, reach + 1)
        ]
        for k in range(breadth):
            acc = None
            for r in range(2 * reach + 1):
                term = rot[pl.ds(offset + r * breadth + k, 1), e] * u[r]
                acc = term if acc is None else acc + term
            out[pl.ds((degree * degree + k) * width, width), e] = acc.astype(BF)


def frame_pairs():
    listing = [(degree, 0) for degree in range(7)]
    for order in (1, 2):
        listing = listing + [(degree, order) for degree in range(order, 7)]
        listing = listing + [(degree, -order) for degree in range(order, 7)]
    return listing


def onehot(ids, rows):
    return (lax.broadcasted_iota(jnp.int32, (rows, ids.shape[1]), 0) == ids).astype(BF)


def onehot_cols(ids, columns):
    return (lax.broadcasted_iota(jnp.int32, (ids.shape[0], columns), 1) == ids).astype(BF)


def prep_kernel(sends, node, cot, send_out, cot_out):
    atoms = node.shape[1]
    send_out[...] = dot(onehot_cols(sends[...], atoms), node[...], NT).astype(BF)
    eye = onehot_cols(lax.broadcasted_iota(jnp.int32, (atoms, 1), 0), atoms)
    cot_out[...] = dot(eye, cot[...], NT).astype(BF)


def frame_kernel(
    node,
    recv,
    cot,
    rotation,
    envelope,
    source,
    target,
    count,
    valid,
    gz,
    g1,
    g2,
    dz_out,
    d1_out,
    d2_out,
    rot,
    raw,
    radial,
    hz,
    h1,
    h2,
):
    atoms = node.shape[1]
    slots = recv.shape[0]
    edges = rotation.shape[1]
    blocks = edges // LANES
    groups = cot.shape[0]
    width = node.shape[0] // 49
    channels = gz.shape[0] // 7
    g12 = {1: g1, 2: g2}
    h12 = {1: h1, 2: h2}

    rot[...] = rotation[...].astype(F32)
    ids = source[...]
    own = onehot(ids, atoms)
    halo = onehot(ids - atoms, slots)
    usable = jnp.sum(halo.astype(F32) * valid[...], axis=0, keepdims=True)
    usable = jnp.where(ids < atoms, 1.0, usable)
    place = lax.broadcasted_iota(jnp.int32, (1, edges), 1)
    radial[...] = jnp.where(place < count[...], envelope[...] * usable, 0.0)
    to = onehot(target[...], atoms)

    def group(q, carry):
        raw[...] = dot(cot[q], to, TN)

        def one(block, carry):
            e = cols(block)
            scale = radial[:, e]

            def put(degree, m, value):
                value = (value * scale).astype(BF)
                order = abs(m)
                row = pl.ds(
                    pl.multiple_of((degree - order) * channels + q * width, width), width
                )
                if order == 0:
                    gz[row, e] = value
                else:
                    g12[order][row, cols(block, 0 if m > 0 else edges)] = value

            rotate_in(rot, raw, block, width, put)
            return carry

        return lax.fori_loop(0, blocks, one, carry)

    lax.fori_loop(0, groups, group, 0)

    raw[...] = dot(node[...], own, NN) + dot(recv[...], halo, TN)
    hz[...] = jnp.zeros_like(hz)
    h2[...] = jnp.zeros_like(h2)

    def one_h(block, carry):
        e = cols(block)
        later = cols(block, edges)

        def put(degree, m, value):
            value = value.astype(BF)
            order = abs(m)
            first = (degree - order) * width
            second = (7 - order + degree - order) * width
            if order == 0:
                hz[pl.ds(first, width), e] = value
            elif m > 0:
                h12[order][pl.ds(first, width), e] = value
                h12[order][pl.ds(second, width), later] = value
            else:
                h12[order][pl.ds(first, width), later] = value
                h12[order][pl.ds(second, width), e] = -value

        rotate_in(rot, raw, block, width, put)
        return carry

    lax.fori_loop(0, blocks, one_h, 0)

    dz_out[...] = dot(gz[...], hz[...], NT)
    d1_out[...] = dot(g1[...], h1[...], NT)
    d2_out[...] = dot(g2[...], h2[...], NT)


def back_kernel(gz, g1, g2, wz, w1, w2, rotation, source, own_out, halo_out, rot, fb, y):
    edges = rotation.shape[1]
    blocks = edges // LANES
    atoms = own_out.shape[1]
    slots = halo_out.shape[0]
    width = wz.shape[0] // 7
    rot[...] = rotation[...].astype(F32)
    fb[pl.ds(0, 7 * width), :] = dot(wz[...], gz[...], NN)
    start = 7 * width
    for count_l, w, g in ((6, w1, g1), (5, w2, g2)):
        rows = count_l * width
        real = dot(w[pl.ds(0, rows), :], g[...], NN)
        imag = dot(w[pl.ds(rows, rows), :], g[...], NN)
        fb[pl.ds(start, rows), :] = real[:, :edges] + imag[:, edges:]
        fb[pl.ds(start + rows, rows), :] = real[:, edges:] - imag[:, :edges]
        start += 2 * rows

    def one(block, carry):
        rotate_out(rot, fb, block, width, y)
        return carry

    lax.fori_loop(0, blocks, one, 0)
    ids = source[...]
    own_out[...] = dot(y[...], onehot(ids, atoms), NT)
    halo_out[...] = dot(onehot(ids - atoms, slots), y[...], NT).astype(BF)


def join_kernel(own, back, sends, out):
    out[...] = own[...] + dot(back[...], onehot_cols(sends[...], own.shape[1]), TN)


def column(row):
    n = row.shape[1]
    diag = lax.broadcasted_iota(jnp.int32, (n, n), 0) == lax.broadcasted_iota(
        jnp.int32, (n, n), 1
    )
    spread = jnp.where(diag, jnp.broadcast_to(row.astype(F32), (n, n)), 0.0)
    return jnp.sum(spread, axis=1, keepdims=True)


def whole_kernel(
    factor,
    sends_in,
    node,
    cot,
    rotation,
    envelope,
    source,
    target,
    count,
    counts_in,
    wz_in,
    w1_in,
    w2_in,
    x_out,
    dz_out,
    d1_out,
    d2_out,
    mine,
    land,
    cots,
    rot,
    raw,
    radial,
    gz,
    g1,
    g2,
    qz,
    q1,
    q2,
    hz,
    h1,
    h2,
    wz,
    w1,
    w2,
    fb,
    y,
    back_mine,
    back_land,
    pieces,
    near,
    passing,
    far,
    total,
    halo_sent,
    halo_got,
    chan_sent,
    chan_got,
    near_sent,
    near_got,
    far_sent,
    far_got,
    back_sent,
    back_got,
):
    parts, halo, rows_x = land.shape
    groups = cots.shape[0]
    atoms = node.shape[1]
    slots = parts * halo
    edges = rotation.shape[1]
    blocks = edges // LANES
    width = rows_x // 49
    channels = width * groups
    share = channels // parts
    me = lax.axis_index("atoms")
    group = lax.axis_index("chan")
    line, side = me // 2, lax.rem(me, 2)
    other = line * 2 + 1 - side

    def push(src, dst, sent, got, where):
        return pltpu.make_async_remote_copy(
            src_ref=src,
            dst_ref=dst,
            send_sem=sent,
            recv_sem=got,
            device_id=where,
            device_id_type=MESH,
        )

    barrier = pltpu.get_barrier_semaphore()
    for k in range(1, parts):
        pl.semaphore_signal(
            barrier, inc=1, device_id={"atoms": lax.rem(me + k, parts)}, device_id_type=MESH
        )
    for k in range(1, groups):
        pl.semaphore_signal(
            barrier, inc=1, device_id={"chan": lax.rem(group + k, groups)}, device_id_type=MESH
        )
    sends = jnp.concatenate([column(sends_in[p : p + 1, :]) for p in range(parts)], axis=0)
    sends = sends.astype(jnp.int32)
    eye = onehot_cols(lax.broadcasted_iota(jnp.int32, (atoms, 1), 0), atoms)
    cots[group] = dot(eye, cot[...], NT).astype(BF)
    picked = dot(onehot_cols(sends, atoms), node[...], NT).astype(BF)
    for p in range(parts):
        mine[p] = picked[p * halo : (p + 1) * halo, :]
    pl.semaphore_wait(barrier, parts + groups - 2)

    halo_copies = []
    for k in range(1, parts):
        peer = lax.rem(me + k, parts)
        copy = push(
            mine.at[peer], land.at[me], halo_sent.at[k], halo_got.at[k], {"atoms": peer}
        )
        copy.start()
        halo_copies.append(copy)
    chan_copies = []
    for k in range(1, groups):
        peer = lax.rem(group + k, groups)
        copy = push(
            cots.at[group], cots.at[group], chan_sent.at[k], chan_got.at[k], {"chan": peer}
        )
        copy.start()
        chan_copies.append(copy)
    land[me] = mine[me]

    rot[...] = rotation[...].astype(F32)
    ids = source[...]
    own = onehot(ids, atoms)
    remote = onehot(ids - atoms, slots)
    order = lax.broadcasted_iota(jnp.int32, (halo, 1), 0)
    valid = jnp.concatenate(
        [(order < counts_in[:, p : p + 1]).astype(F32) for p in range(parts)], axis=0
    )
    usable = jnp.sum(remote.astype(F32) * valid, axis=0, keepdims=True)
    usable = jnp.where(ids < atoms, 1.0, usable)
    place = lax.broadcasted_iota(jnp.int32, (1, edges), 1)
    radial[...] = jnp.where(place < count[...], envelope[...] * usable, 0.0)
    to = onehot(target[...], atoms)

    g12 = {1: g1, 2: g2}
    q12 = {1: q1, 2: q2}
    h12 = {1: h1, 2: h2}

    def frame_grad(q):
        raw[...] = dot(cots[q], to, TN)

        def one(block, carry):
            e = cols(block)
            scale = radial[:, e]

            def put(degree, m, value):
                value = (value * scale).astype(BF)
                o = abs(m)
                row = pl.ds(
                    pl.multiple_of((degree - o) * channels + q * width, width), width
                )
                short = pl.ds((degree - o) * width, width)
                if o == 0:
                    gz[row, e] = value
                    qz[short, e] = value
                else:
                    at = cols(block, 0 if m > 0 else edges)
                    g12[o][row, at] = value
                    q12[o][short, at] = value

            rotate_in(rot, raw, block, width, put)
            return carry

        lax.fori_loop(0, blocks, one, 0)

    def one_h(block, carry):
        e = cols(block)
        later = cols(block, edges)

        def put(degree, m, value):
            value = value.astype(BF)
            o = abs(m)
            first = (degree - o) * width
            second = (7 - o + degree - o) * width
            if o == 0:
                hz[pl.ds(first, width), e] = value
            elif m > 0:
                h12[o][pl.ds(first, width), e] = value
                h12[o][pl.ds(second, width), later] = value
            else:
                h12[o][pl.ds(first, width), later] = value
                h12[o][pl.ds(second, width), e] = -value

        rotate_in(rot, raw, block, width, put)
        return carry

    near_copies = []

    def weight_piece(k):
        base = 0
        for count_l, g, h in ((7, qz, hz), (6, q1, h1), (5, q2, h2)):
            part = dot(g[...], h[...], NT).astype(BF)
            tiles = h.shape[0] // LANES
            for tile in range(tiles):
                for degree in range(count_l):
                    start = base + (tile * count_l + degree) * share
                    for half in range(2):
                        row = degree * width + half * share
                        pieces[k, half, start : start + share, :] = part[
                            row : row + share, tile * LANES : (tile + 1) * LANES
                        ]
            base += tiles * count_l * share
        copy = push(
            pieces.at[k, 1 - side],
            near.at[k],
            near_sent.at[k],
            near_got.at[k],
            {"atoms": other},
        )
        copy.start()
        near_copies.append(copy)

    def far_copy(k, q):
        slot = lax.rem(line - q + groups + groups - 1, groups)
        return push(
            passing.at[k],
            far.at[slot],
            far_sent.at[k],
            far_got.at[slot],
            {"atoms": q * 2 + side},
        )

    def pass_on(k):
        near_copies[k].wait_recv()
        q = lax.rem(group + k, groups)
        value = pieces[k, side].astype(F32) + near[k].astype(F32)

        @pl.when(q == line)
        def keep():
            total[...] = value

        @pl.when(q != line)
        def send():
            passing[k] = value.astype(BF)
            far_copy(k, q).start()

    frame_grad(group)
    for copy in halo_copies:
        copy.wait_recv()
    hz[...] = jnp.zeros_like(hz)
    h2[...] = jnp.zeros_like(h2)
    table = land[...].astype(F32).reshape(slots, rows_x).astype(BF)
    raw[...] = dot(node[...], own, NN) + dot(table, remote, TN)
    lax.fori_loop(0, blocks, one_h, 0)
    weight_piece(0)

    for i in range(7):
        for j in range(7):
            wz[i * width : (i + 1) * width, j * channels : (j + 1) * channels] = wz_in[i, j]
    for count_l, w, w_in in ((6, w1, w1_in), (5, w2, w2_in)):
        for part in range(2):
            for i in range(count_l):
                for j in range(count_l):
                    at = (part * count_l + i) * width
                    w[at : at + width, j * channels : (j + 1) * channels] = w_in[part, i, j]

    for k in range(1, groups):
        chan_copies[groups - k - 1].wait_recv()
        frame_grad(lax.rem(group + k, groups))
        weight_piece(k)
        pass_on(k - 1)

    fb[pl.ds(0, 7 * width), :] = dot(wz[...], gz[...], NN)
    start = 7 * width
    for count_l, w, g in ((6, w1, g1), (5, w2, g2)):
        rows = count_l * width
        real = dot(w[pl.ds(0, rows), :], g[...], NN)
        imag = dot(w[pl.ds(rows, rows), :], g[...], NN)
        fb[pl.ds(start, rows), :] = real[:, :edges] + imag[:, edges:]
        fb[pl.ds(start + rows, rows), :] = real[:, edges:] - imag[:, :edges]
        start += 2 * rows
    pass_on(groups - 1)

    def one_back(block, carry):
        rotate_out(rot, fb, block, width, y)
        return carry

    lax.fori_loop(0, blocks, one_back, 0)
    terms = dot(remote, y[...], NT).astype(BF)
    for p in range(parts):
        back_mine[p] = terms[p * halo : (p + 1) * halo, :]
    back_copies = []
    for k in range(1, parts):
        peer = lax.rem(me + k, parts)
        copy = push(
            back_mine.at[peer],
            back_land.at[me],
            back_sent.at[k],
            back_got.at[k],
            {"atoms": peer},
        )
        copy.start()
        back_copies.append(copy)
    back_land[me] = back_mine[me]
    x_out[...] = dot(y[...], own, NT)

    value = total[...]
    for j in range(groups - 1):
        push(
            passing.at[0], far.at[j], far_sent.at[0], far_got.at[j], {"atoms": other}
        ).wait_recv()
        value = value + far[j].astype(F32)
    total[...] = value * factor
    base = 0
    for c, (count_l, h, out) in enumerate(((7, hz, dz_out), (6, h1, d1_out), (5, h2, d2_out))):
        for i in range(count_l if c == 0 else 2 * count_l):
            tile, lane = divmod(i * width, LANES)
            for j in range(count_l):
                row = base + (tile * count_l + j) * share
                cut = total[row : row + share, lane : lane + width]
                if c == 0:
                    out[i, j] = cut
                else:
                    out[i // count_l, i % count_l, j] = cut
        base += h.shape[0] // LANES * count_l * share

    for copy in back_copies:
        copy.wait_recv()
    returned = back_land[...].astype(F32).reshape(slots, rows_x).astype(BF)
    x_out[...] += dot(returned, onehot_cols(sends, atoms), TN)

    for copy in halo_copies + chan_copies + near_copies + back_copies:
        copy.wait_send()
    for k in range(groups):
        q = lax.rem(group + k, groups)

        @pl.when(q != line)
        def drain():
            far_copy(k, q).wait_send()


def call(kernel, outs, scratch=(), flops=10**8, collective=None):
    if collective is None:
        params = pltpu.CompilerParams(vmem_limit_bytes=VMEM_LIMIT)
    else:
        params = pltpu.CompilerParams(
            vmem_limit_bytes=VMEM_LIMIT, collective_id=collective, has_side_effects=True
        )
    return pl.pallas_call(
        kernel,
        out_shape=outs,
        scratch_shapes=list(scratch),
        compiler_params=params,
        cost_estimate=pl.CostEstimate(
            flops=flops, bytes_accessed=8 * 10**6, transcendentals=0
        ),
    )


def on_device(
    node_x,
    cotangent,
    rotation,
    envelope,
    source,
    target,
    edge_count,
    send_index,
    halo_count,
    weight_zero,
    weight_one,
    weight_two,
):
    parts = lax.axis_size("atoms")
    groups = lax.axis_size("chan")
    width = node_x.shape[1]
    channels = width * groups
    atoms = node_x.shape[2]
    halo = send_index.shape[2]
    edges = source.shape[0]
    slots = parts * halo
    rows = 49 * width
    share = channels // parts
    fast = parts == 2 * groups and share % 16 == 0 and width == 2 * share
    sds = jax.ShapeDtypeStruct

    node = node_x.reshape(rows, atoms)
    cot = cotangent.reshape(rows, atoms)
    factor = 1.0 / math.sqrt(edges * parts)
    src = source.reshape(1, edges)
    tgt = target.reshape(1, edges)
    pad = lambda n: -(-n // LANES) * LANES
    lz, l1, l2 = pad(7 * width), pad(12 * width), pad(10 * width)

    if fast:
        height = (7 * lz + 6 * l1 + 5 * l2) // LANES * share
        vmem = pltpu.VMEM
        dma = pltpu.SemaphoreType.DMA
        grad_x, dz, d1, d2 = call(
            functools.partial(whole_kernel, factor),
            (
                sds((rows, atoms), F32),
                sds((7, 7, share, width), F32),
                sds((2, 6, 6, share, width), F32),
                sds((2, 5, 5, share, width), F32),
            ),
            (
                vmem((parts, halo, rows), BF),
                vmem((parts, halo, rows), BF),
                vmem((groups, atoms, rows), BF),
                vmem((235, edges), F32),
                vmem((rows, edges), F32),
                vmem((1, edges), F32),
                vmem((7 * channels, edges), BF),
                vmem((6 * channels, 2 * edges), BF),
                vmem((5 * channels, 2 * edges), BF),
                vmem((7 * width, edges), BF),
                vmem((6 * width, 2 * edges), BF),
                vmem((5 * width, 2 * edges), BF),
                vmem((lz, edges), BF),
                vmem((l1, 2 * edges), BF),
                vmem((l2, 2 * edges), BF),
                vmem((7 * width, 7 * channels), BF),
                vmem((12 * width, 6 * channels), BF),
                vmem((10 * width, 5 * channels), BF),
                vmem((29 * width, edges), F32),
                vmem((rows, edges), BF),
                vmem((parts, halo, rows), BF),
                vmem((parts, halo, rows), BF),
                vmem((groups, 2, height, LANES), BF),
                vmem((groups, height, LANES), BF),
                vmem((groups, height, LANES), BF),
                vmem((groups - 1, height, LANES), BF),
                vmem((height, LANES), F32),
                dma((parts,)),
                dma((parts,)),
                dma((groups,)),
                dma((groups,)),
                dma((groups,)),
                dma((groups,)),
                dma((groups,)),
                dma((groups - 1,)),
                dma((parts,)),
                dma((parts,)),
            ),
            flops=10**10,
            collective=0,
        )(
            send_index[0],
            node,
            cot,
            rotation,
            envelope.reshape(1, edges),
            src,
            tgt,
            edge_count.reshape(1, 1),
            halo_count.reshape(1, parts),
            weight_zero.transpose(0, 2, 1, 3),
            weight_one.transpose(0, 1, 3, 2, 4),
            weight_two.transpose(0, 1, 3, 2, 4),
        )
        return (
            grad_x.reshape(49, width, atoms),
            dz.transpose(0, 3, 1, 2),
            d1.transpose(0, 1, 4, 2, 3),
            d2.transpose(0, 1, 4, 2, 3),
        )

    sends = send_index.reshape(slots, 1)
    send_rows, cot_rows = call(
        prep_kernel, (sds((slots, rows), BF), sds((atoms, rows), BF))
    )(sends, node, cot)
    recv = lax.all_to_all(send_rows, "atoms", split_axis=0, concat_axis=0, tiled=True)
    cots = lax.all_gather(cot_rows, "chan", axis=0, tiled=False)
    valid = (
        jnp.arange(halo, dtype=jnp.int32)[None, :] < halo_count[:, 0][:, None]
    ).astype(F32).reshape(slots, 1)
    g_shapes = (
        sds((7 * channels, edges), BF),
        sds((6 * channels, 2 * edges), BF),
        sds((5 * channels, 2 * edges), BF),
    )
    d_shapes = (
        sds((7 * channels, lz), F32),
        sds((6 * channels, l1), F32),
        sds((5 * channels, l2), F32),
    )
    made = call(
        frame_kernel,
        g_shapes + d_shapes,
        (
            pltpu.VMEM((235, edges), F32),
            pltpu.VMEM((rows, edges), F32),
            pltpu.VMEM((1, edges), F32),
            pltpu.VMEM((lz, edges), BF),
            pltpu.VMEM((l1, 2 * edges), BF),
            pltpu.VMEM((l2, 2 * edges), BF),
        ),
        flops=10**10,
    )(
        node,
        recv,
        cots,
        rotation,
        envelope.reshape(1, edges),
        src,
        tgt,
        edge_count.reshape(1, 1),
        valid,
    )
    gz, g1, g2 = made[:3]
    own, halo_rows = call(
        back_kernel,
        (sds((rows, atoms), F32), sds((slots, rows), BF)),
        (
            pltpu.VMEM((235, edges), F32),
            pltpu.VMEM((29 * width, edges), F32),
            pltpu.VMEM((rows, edges), BF),
        ),
        flops=10**10,
    )(
        gz,
        g1,
        g2,
        weight_zero.reshape(7 * width, 7 * channels),
        weight_one.reshape(12 * width, 6 * channels),
        weight_two.reshape(10 * width, 5 * channels),
        rotation,
        src,
    )
    back = lax.all_to_all(halo_rows, "atoms", split_axis=0, concat_axis=0, tiled=True)
    grad_x = call(join_kernel, sds((rows, atoms), F32))(own, back, sends)

    dz = made[3][:, : 7 * width].reshape(7, channels, 7, width)
    d1 = made[4].reshape(6, channels, 2, 6, width)
    d2 = made[5][:, : 10 * width].reshape(5, channels, 2, 5, width)
    dz = lax.psum_scatter(dz, "atoms", scatter_dimension=1, tiled=True)
    d1 = lax.psum_scatter(d1, "atoms", scatter_dimension=1, tiled=True)
    d2 = lax.psum_scatter(d2, "atoms", scatter_dimension=1, tiled=True)
    return (
        grad_x.reshape(49, width, atoms),
        dz.transpose(2, 3, 0, 1) * factor,
        d1.transpose(2, 3, 4, 0, 1) * factor,
        d2.transpose(2, 3, 4, 0, 1) * factor,
    )


def solution(mesh):
    in_specs = (
        P(None, "chan", "atoms"),
        P(None, "chan", "atoms"),
        P(None, "atoms"),
        P("atoms"),
        P("atoms"),
        P("atoms"),
        P("atoms"),
        P("atoms", None, None),
        P(None, "atoms"),
        P(None, "chan", None, None),
        P(None, None, "chan", None, None),
        P(None, None, "chan", None, None),
    )
    out_specs = (
        P(None, "chan", "atoms"),
        P(None, "chan", None, "atoms"),
        P(None, None, "chan", None, "atoms"),
        P(None, None, "chan", None, "atoms"),
    )
    return jax.shard_map(
        on_device, mesh=mesh, in_specs=in_specs, out_specs=out_specs, check_vma=False
    )
```

```python
import functools
import math

import jax
import jax.numpy as jnp
from jax import lax
from jax.experimental import pallas as pl
from jax.experimental.pallas import tpu as pltpu
from jax.sharding import PartitionSpec as P

LANES = 128
BF = jnp.bfloat16
F32 = jnp.float32
VMEM_LIMIT = 56 * 1024 * 1024
MESH = pl.DeviceIdType.MESH


def dot(a, b, dims):
    return lax.dot_general(a, b, (dims, ((), ())), preferred_element_type=F32)


NN = ((1,), (0,))
NT = ((1,), (1,))
TN = ((0,), (0,))


def degrees():
    offset = 0
    for degree in range(7):
        reach = min(degree, 2)
        yield degree, reach, offset
        offset += (2 * reach + 1) * (2 * degree + 1)


def cols(block, base=0):
    return pl.ds(pl.multiple_of(base + block * LANES, LANES), LANES)


def rotate_in(rot, raw, block, width, put):
    e = cols(block)
    for degree, reach, offset in degrees():
        breadth = 2 * degree + 1
        acc = [None] * (2 * reach + 1)
        for k in range(breadth):
            v = raw[pl.ds((degree * degree + k) * width, width), e]
            for r in range(2 * reach + 1):
                term = rot[pl.ds(offset + r * breadth + k, 1), e] * v
                acc[r] = term if acc[r] is None else acc[r] + term
        for r in range(2 * reach + 1):
            put(degree, r - reach, acc[r])


def rotate_out(rot, framed, block, width, out):
    e = cols(block)
    spots = {}
    for i, pair in enumerate(frame_pairs()):
        spots[pair] = i
    for degree, reach, offset in degrees():
        breadth = 2 * degree + 1
        u = [
            framed[pl.ds(spots[degree, m] * width, width), e]
            for m in range(-reach, reach + 1)
        ]
        for k in range(breadth):
            acc = None
            for r in range(2 * reach + 1):
                term = rot[pl.ds(offset + r * breadth + k, 1), e] * u[r]
                acc = term if acc is None else acc + term
            out[pl.ds((degree * degree + k) * width, width), e] = acc.astype(BF)


def frame_pairs():
    listing = [(degree, 0) for degree in range(7)]
    for order in (1, 2):
        listing = listing + [(degree, order) for degree in range(order, 7)]
        listing = listing + [(degree, -order) for degree in range(order, 7)]
    return listing


def onehot(ids, rows):
    return (lax.broadcasted_iota(jnp.int32, (rows, ids.shape[1]), 0) == ids).astype(BF)


def onehot_cols(ids, columns):
    return (lax.broadcasted_iota(jnp.int32, (ids.shape[0], columns), 1) == ids).astype(BF)


def prep_kernel(sends, node, cot, send_out, cot_out):
    atoms = node.shape[1]
    send_out[...] = dot(onehot_cols(sends[...], atoms), node[...], NT).astype(BF)
    eye = onehot_cols(lax.broadcasted_iota(jnp.int32, (atoms, 1), 0), atoms)
    cot_out[...] = dot(eye, cot[...], NT).astype(BF)


def frame_kernel(
    node,
    recv,
    cot,
    rotation,
    envelope,
    source,
    target,
    count,
    valid,
    gz,
    g1,
    g2,
    dz_out,
    d1_out,
    d2_out,
    rot,
    raw,
    radial,
    hz,
    h1,
    h2,
):
    atoms = node.shape[1]
    slots = recv.shape[0]
    edges = rotation.shape[1]
    blocks = edges // LANES
    groups = cot.shape[0]
    width = node.shape[0] // 49
    channels = gz.shape[0] // 7
    g12 = {1: g1, 2: g2}
    h12 = {1: h1, 2: h2}

    rot[...] = rotation[...].astype(F32)
    ids = source[...]
    own = onehot(ids, atoms)
    halo = onehot(ids - atoms, slots)
    usable = jnp.sum(halo.astype(F32) * valid[...], axis=0, keepdims=True)
    usable = jnp.where(ids < atoms, 1.0, usable)
    place = lax.broadcasted_iota(jnp.int32, (1, edges), 1)
    radial[...] = jnp.where(place < count[...], envelope[...] * usable, 0.0)
    to = onehot(target[...], atoms)

    def group(q, carry):
        raw[...] = dot(cot[q], to, TN)

        def one(block, carry):
            e = cols(block)
            scale = radial[:, e]

            def put(degree, m, value):
                value = (value * scale).astype(BF)
                order = abs(m)
                row = pl.ds(
                    pl.multiple_of((degree - order) * channels + q * width, width), width
                )
                if order == 0:
                    gz[row, e] = value
                else:
                    g12[order][row, cols(block, 0 if m > 0 else edges)] = value

            rotate_in(rot, raw, block, width, put)
            return carry

        return lax.fori_loop(0, blocks, one, carry)

    lax.fori_loop(0, groups, group, 0)

    raw[...] = dot(node[...], own, NN) + dot(recv[...], halo, TN)
    hz[...] = jnp.zeros_like(hz)
    h2[...] = jnp.zeros_like(h2)

    def one_h(block, carry):
        e = cols(block)
        later = cols(block, edges)

        def put(degree, m, value):
            value = value.astype(BF)
            order = abs(m)
            first = (degree - order) * width
            second = (7 - order + degree - order) * width
            if order == 0:
                hz[pl.ds(first, width), e] = value
            elif m > 0:
                h12[order][pl.ds(first, width), e] = value
                h12[order][pl.ds(second, width), later] = value
            else:
                h12[order][pl.ds(first, width), later] = value
                h12[order][pl.ds(second, width), e] = -value

        rotate_in(rot, raw, block, width, put)
        return carry

    lax.fori_loop(0, blocks, one_h, 0)

    dz_out[...] = dot(gz[...], hz[...], NT)
    d1_out[...] = dot(g1[...], h1[...], NT)
    d2_out[...] = dot(g2[...], h2[...], NT)


def back_kernel(gz, g1, g2, wz, w1, w2, rotation, source, own_out, halo_out, rot, fb, y):
    edges = rotation.shape[1]
    blocks = edges // LANES
    atoms = own_out.shape[1]
    slots = halo_out.shape[0]
    width = wz.shape[0] // 7
    rot[...] = rotation[...].astype(F32)
    fb[pl.ds(0, 7 * width), :] = dot(wz[...], gz[...], NN)
    start = 7 * width
    for count_l, w, g in ((6, w1, g1), (5, w2, g2)):
        rows = count_l * width
        real = dot(w[pl.ds(0, rows), :], g[...], NN)
        imag = dot(w[pl.ds(rows, rows), :], g[...], NN)
        fb[pl.ds(start, rows), :] = real[:, :edges] + imag[:, edges:]
        fb[pl.ds(start + rows, rows), :] = real[:, edges:] - imag[:, :edges]
        start += 2 * rows

    def one(block, carry):
        rotate_out(rot, fb, block, width, y)
        return carry

    lax.fori_loop(0, blocks, one, 0)
    ids = source[...]
    own_out[...] = dot(y[...], onehot(ids, atoms), NT)
    halo_out[...] = dot(onehot(ids - atoms, slots), y[...], NT).astype(BF)


def join_kernel(own, back, sends, out):
    out[...] = own[...] + dot(back[...], onehot_cols(sends[...], own.shape[1]), TN)


def column(row):
    n = row.shape[1]
    diag = lax.broadcasted_iota(jnp.int32, (n, n), 0) == lax.broadcasted_iota(
        jnp.int32, (n, n), 1
    )
    spread = jnp.where(diag, jnp.broadcast_to(row.astype(F32), (n, n)), 0.0)
    return jnp.sum(spread, axis=1, keepdims=True)


def whole_kernel(
    factor,
    sends_in,
    node,
    cot,
    rotation,
    envelope,
    source,
    target,
    count,
    counts_in,
    wz_in,
    w1_in,
    w2_in,
    x_out,
    total,
    mine,
    land,
    cots,
    rot,
    raw,
    radial,
    gz,
    g1,
    g2,
    qz,
    q1,
    q2,
    hz,
    h1,
    h2,
    wz,
    w1,
    w2,
    fb,
    y,
    back_mine,
    back_land,
    pieces,
    near,
    passing,
    far,
    halo_sent,
    halo_got,
    chan_sent,
    chan_got,
    near_sent,
    near_got,
    far_sent,
    far_got,
    back_sent,
    back_got,
):
    parts, halo, rows_x = land.shape
    groups = cots.shape[0]
    atoms = node.shape[1]
    slots = parts * halo
    edges = rotation.shape[1]
    blocks = edges // LANES
    width = rows_x // 49
    channels = width * groups
    share = channels // parts
    me = lax.axis_index("atoms")
    group = lax.axis_index("chan")
    line, side = me // 2, lax.rem(me, 2)
    other = line * 2 + 1 - side

    def push(src, dst, sent, got, where):
        return pltpu.make_async_remote_copy(
            src_ref=src,
            dst_ref=dst,
            send_sem=sent,
            recv_sem=got,
            device_id=where,
            device_id_type=MESH,
        )

    barrier = pltpu.get_barrier_semaphore()
    for k in range(1, parts):
        pl.semaphore_signal(
            barrier, inc=1, device_id={"atoms": lax.rem(me + k, parts)}, device_id_type=MESH
        )
    for k in range(1, groups):
        pl.semaphore_signal(
            barrier, inc=1, device_id={"chan": lax.rem(group + k, groups)}, device_id_type=MESH
        )
    sends = jnp.concatenate([column(sends_in[p : p + 1, :]) for p in range(parts)], axis=0)
    sends = sends.astype(jnp.int32)
    eye = onehot_cols(lax.broadcasted_iota(jnp.int32, (atoms, 1), 0), atoms)
    cots[group] = dot(eye, cot[...], NT).astype(BF)
    picked = dot(onehot_cols(sends, atoms), node[...], NT).astype(BF)
    for p in range(parts):
        mine[p] = picked[p * halo : (p + 1) * halo, :]
    pl.semaphore_wait(barrier, parts + groups - 2)

    halo_copies = []
    for k in range(1, parts):
        peer = lax.rem(me + k, parts)
        copy = push(
            mine.at[peer], land.at[me], halo_sent.at[k], halo_got.at[k], {"atoms": peer}
        )
        copy.start()
        halo_copies.append(copy)
    chan_copies = []
    for k in range(1, groups):
        peer = lax.rem(group + k, groups)
        copy = push(
            cots.at[group], cots.at[group], chan_sent.at[k], chan_got.at[k], {"chan": peer}
        )
        copy.start()
        chan_copies.append(copy)
    land[me] = mine[me]

    rot[...] = rotation[...].astype(F32)
    ids = source[...]
    own = onehot(ids, atoms)
    remote = onehot(ids - atoms, slots)
    order = lax.broadcasted_iota(jnp.int32, (halo, 1), 0)
    valid = jnp.concatenate(
        [(order < counts_in[:, p : p + 1]).astype(F32) for p in range(parts)], axis=0
    )
    usable = jnp.sum(remote.astype(F32) * valid, axis=0, keepdims=True)
    usable = jnp.where(ids < atoms, 1.0, usable)
    place = lax.broadcasted_iota(jnp.int32, (1, edges), 1)
    radial[...] = jnp.where(place < count[...], envelope[...] * usable, 0.0)
    to = onehot(target[...], atoms)

    g12 = {1: g1, 2: g2}
    q12 = {1: q1, 2: q2}
    h12 = {1: h1, 2: h2}

    def frame_grad(q):
        raw[...] = dot(cots[q], to, TN)

        def one(block, carry):
            e = cols(block)
            scale = radial[:, e]

            def put(degree, m, value):
                value = (value * scale).astype(BF)
                o = abs(m)
                row = pl.ds(
                    pl.multiple_of((degree - o) * channels + q * width, width), width
                )
                short = pl.ds((degree - o) * width, width)
                if o == 0:
                    gz[row, e] = value
                    qz[short, e] = value
                else:
                    at = cols(block, 0 if m > 0 else edges)
                    g12[o][row, at] = value
                    q12[o][short, at] = value

            rotate_in(rot, raw, block, width, put)
            return carry

        lax.fori_loop(0, blocks, one, 0)

    def one_h(block, carry):
        e = cols(block)
        later = cols(block, edges)

        def put(degree, m, value):
            value = value.astype(BF)
            o = abs(m)
            first = (degree - o) * width
            second = (7 - o + degree - o) * width
            if o == 0:
                hz[pl.ds(first, width), e] = value
            elif m > 0:
                h12[o][pl.ds(first, width), e] = value
                h12[o][pl.ds(second, width), later] = value
            else:
                h12[o][pl.ds(first, width), later] = value
                h12[o][pl.ds(second, width), e] = -value

        rotate_in(rot, raw, block, width, put)
        return carry

    near_copies = []

    def weight_piece(k):
        base = 0
        for count_l, g, h in ((7, qz, hz), (6, q1, h1), (5, q2, h2)):
            part = dot(g[...], h[...], NT).astype(BF)
            tiles = h.shape[0] // LANES
            for tile in range(tiles):
                for degree in range(count_l):
                    start = base + (tile * count_l + degree) * share
                    for half in range(2):
                        row = degree * width + half * share
                        pieces[k, half, start : start + share, :] = part[
                            row : row + share, tile * LANES : (tile + 1) * LANES
                        ]
            base += tiles * count_l * share
        copy = push(
            pieces.at[k, 1 - side],
            near.at[k],
            near_sent.at[k],
            near_got.at[k],
            {"atoms": other},
        )
        copy.start()
        near_copies.append(copy)

    def far_copy(k, q):
        slot = lax.rem(line - q + groups + groups - 1, groups)
        return push(
            passing.at[k],
            far.at[slot],
            far_sent.at[k],
            far_got.at[slot],
            {"atoms": q * 2 + side},
        )

    def pass_on(k):
        near_copies[k].wait_recv()
        q = lax.rem(group + k, groups)
        value = pieces[k, side].astype(F32) + near[k].astype(F32)

        @pl.when(q == line)
        def keep():
            total[...] = value

        @pl.when(q != line)
        def send():
            passing[k] = value.astype(BF)
            far_copy(k, q).start()

    frame_grad(group)
    for copy in halo_copies:
        copy.wait_recv()
    hz[...] = jnp.zeros_like(hz)
    h2[...] = jnp.zeros_like(h2)
    table = land[...].astype(F32).reshape(slots, rows_x).astype(BF)
    raw[...] = dot(node[...], own, NN) + dot(table, remote, TN)
    lax.fori_loop(0, blocks, one_h, 0)
    weight_piece(0)

    for i in range(7):
        for j in range(7):
            wz[i * width : (i + 1) * width, j * channels : (j + 1) * channels] = wz_in[i, j]
    for count_l, w, w_in in ((6, w1, w1_in), (5, w2, w2_in)):
        for part in range(2):
            for i in range(count_l):
                for j in range(count_l):
                    at = (part * count_l + i) * width
                    w[at : at + width, j * channels : (j + 1) * channels] = w_in[part, i, j]

    for k in range(1, groups):
        chan_copies[groups - k - 1].wait_recv()
        frame_grad(lax.rem(group + k, groups))
        weight_piece(k)
        pass_on(k - 1)

    fb[pl.ds(0, 7 * width), :] = dot(wz[...], gz[...], NN)
    start = 7 * width
    for count_l, w, g in ((6, w1, g1), (5, w2, g2)):
        rows = count_l * width
        real = dot(w[pl.ds(0, rows), :], g[...], NN)
        imag = dot(w[pl.ds(rows, rows), :], g[...], NN)
        fb[pl.ds(start, rows), :] = real[:, :edges] + imag[:, edges:]
        fb[pl.ds(start + rows, rows), :] = real[:, edges:] - imag[:, :edges]
        start += 2 * rows

    def one_back(block, carry):
        rotate_out(rot, fb, block, width, y)
        return carry

    lax.fori_loop(0, blocks // 2, one_back, 0)
    pass_on(groups - 1)
    lax.fori_loop(blocks // 2, blocks, one_back, 0)
    terms = dot(remote, y[...], NT).astype(BF)
    for p in range(parts):
        back_mine[p] = terms[p * halo : (p + 1) * halo, :]
    back_copies = []
    for k in range(1, parts):
        peer = lax.rem(me + k, parts)
        copy = push(
            back_mine.at[peer],
            back_land.at[me],
            back_sent.at[k],
            back_got.at[k],
            {"atoms": peer},
        )
        copy.start()
        back_copies.append(copy)
    back_land[me] = back_mine[me]
    x_out[...] = dot(y[...], own, NT)

    value = total[...]
    for j in range(groups - 1):
        push(
            passing.at[0], far.at[j], far_sent.at[0], far_got.at[j], {"atoms": other}
        ).wait_recv()
        value = value + far[j].astype(F32)
    total[...] = value * factor

    for copy in back_copies:
        copy.wait_recv()
    returned = back_land[...].astype(F32).reshape(slots, rows_x).astype(BF)
    x_out[...] += dot(returned, onehot_cols(sends, atoms), TN)

    for copy in halo_copies + chan_copies + near_copies + back_copies:
        copy.wait_send()
    for k in range(groups):
        q = lax.rem(group + k, groups)

        @pl.when(q != line)
        def drain():
            far_copy(k, q).wait_send()


def write_kernel(x, total, x_out, dz_out, d1_out, d2_out):
    x_out[...] = x[...]
    base = 0
    for c, out in enumerate((dz_out, d1_out, d2_out)):
        share, width = out.shape[-2:]
        count_l = 7 - c
        high = count_l if c == 0 else 2 * count_l
        for i in range(high):
            tile, lane = divmod(i * width, LANES)
            for j in range(count_l):
                row = base + (tile * count_l + j) * share
                cut = total[row : row + share, lane : lane + width]
                if c == 0:
                    out[i, j] = cut
                else:
                    out[i // count_l, i % count_l, j] = cut
        base += -(-high * width // LANES) * count_l * share


def call(kernel, outs, scratch=(), flops=10**8, collective=None):
    if collective is None:
        params = pltpu.CompilerParams(vmem_limit_bytes=VMEM_LIMIT)
    else:
        params = pltpu.CompilerParams(
            vmem_limit_bytes=VMEM_LIMIT, collective_id=collective, has_side_effects=True
        )
    return pl.pallas_call(
        kernel,
        out_shape=outs,
        scratch_shapes=list(scratch),
        compiler_params=params,
        cost_estimate=pl.CostEstimate(
            flops=flops, bytes_accessed=8 * 10**6, transcendentals=0
        ),
    )


def on_device(
    node_x,
    cotangent,
    rotation,
    envelope,
    source,
    target,
    edge_count,
    send_index,
    halo_count,
    weight_zero,
    weight_one,
    weight_two,
):
    parts = lax.axis_size("atoms")
    groups = lax.axis_size("chan")
    width = node_x.shape[1]
    channels = width * groups
    atoms = node_x.shape[2]
    halo = send_index.shape[2]
    edges = source.shape[0]
    slots = parts * halo
    rows = 49 * width
    share = channels // parts
    fast = parts == 2 * groups and share % 16 == 0 and width == 2 * share
    sds = jax.ShapeDtypeStruct

    node = node_x.reshape(rows, atoms)
    cot = cotangent.reshape(rows, atoms)
    factor = 1.0 / math.sqrt(edges * parts)
    src = source.reshape(1, edges)
    tgt = target.reshape(1, edges)
    pad = lambda n: -(-n // LANES) * LANES
    lz, l1, l2 = pad(7 * width), pad(12 * width), pad(10 * width)

    if fast:
        height = (7 * lz + 6 * l1 + 5 * l2) // LANES * share
        vmem = pltpu.VMEM
        dma = pltpu.SemaphoreType.DMA
        grad_x, summed = call(
            functools.partial(whole_kernel, factor),
            (sds((rows, atoms), F32), sds((height, LANES), F32)),
            (
                vmem((parts, halo, rows), BF),
                vmem((parts, halo, rows), BF),
                vmem((groups, atoms, rows), BF),
                vmem((235, edges), F32),
                vmem((rows, edges), F32),
                vmem((1, edges), F32),
                vmem((7 * channels, edges), BF),
                vmem((6 * channels, 2 * edges), BF),
                vmem((5 * channels, 2 * edges), BF),
                vmem((7 * width, edges), BF),
                vmem((6 * width, 2 * edges), BF),
                vmem((5 * width, 2 * edges), BF),
                vmem((lz, edges), BF),
                vmem((l1, 2 * edges), BF),
                vmem((l2, 2 * edges), BF),
                vmem((7 * width, 7 * channels), BF),
                vmem((12 * width, 6 * channels), BF),
                vmem((10 * width, 5 * channels), BF),
                vmem((29 * width, edges), F32),
                vmem((rows, edges), BF),
                vmem((parts, halo, rows), BF),
                vmem((parts, halo, rows), BF),
                vmem((groups, 2, height, LANES), BF),
                vmem((groups, height, LANES), BF),
                vmem((groups, height, LANES), BF),
                vmem((groups - 1, height, LANES), BF),
                dma((parts,)),
                dma((parts,)),
                dma((groups,)),
                dma((groups,)),
                dma((groups,)),
                dma((groups,)),
                dma((groups,)),
                dma((groups - 1,)),
                dma((parts,)),
                dma((parts,)),
            ),
            flops=10**10,
            collective=0,
        )(
            send_index[0],
            node,
            cot,
            rotation,
            envelope.reshape(1, edges),
            src,
            tgt,
            edge_count.reshape(1, 1),
            halo_count.reshape(1, parts),
            weight_zero.transpose(0, 2, 1, 3),
            weight_one.transpose(0, 1, 3, 2, 4),
            weight_two.transpose(0, 1, 3, 2, 4),
        )
        grad_x, dz, d1, d2 = call(
            write_kernel,
            (
                sds((rows, atoms), F32),
                sds((7, 7, share, width), F32),
                sds((2, 6, 6, share, width), F32),
                sds((2, 5, 5, share, width), F32),
            ),
        )(grad_x, summed)
        return (
            grad_x.reshape(49, width, atoms),
            dz.transpose(0, 3, 1, 2),
            d1.transpose(0, 1, 4, 2, 3),
            d2.transpose(0, 1, 4, 2, 3),
        )

    sends = send_index.reshape(slots, 1)
    send_rows, cot_rows = call(
        prep_kernel, (sds((slots, rows), BF), sds((atoms, rows), BF))
    )(sends, node, cot)
    recv = lax.all_to_all(send_rows, "atoms", split_axis=0, concat_axis=0, tiled=True)
    cots = lax.all_gather(cot_rows, "chan", axis=0, tiled=False)
    valid = (
        jnp.arange(halo, dtype=jnp.int32)[None, :] < halo_count[:, 0][:, None]
    ).astype(F32).reshape(slots, 1)
    g_shapes = (
        sds((7 * channels, edges), BF),
        sds((6 * channels, 2 * edges), BF),
        sds((5 * channels, 2 * edges), BF),
    )
    d_shapes = (
        sds((7 * channels, lz), F32),
        sds((6 * channels, l1), F32),
        sds((5 * channels, l2), F32),
    )
    made = call(
        frame_kernel,
        g_shapes + d_shapes,
        (
            pltpu.VMEM((235, edges), F32),
            pltpu.VMEM((rows, edges), F32),
            pltpu.VMEM((1, edges), F32),
            pltpu.VMEM((lz, edges), BF),
            pltpu.VMEM((l1, 2 * edges), BF),
            pltpu.VMEM((l2, 2 * edges), BF),
        ),
        flops=10**10,
    )(
        node,
        recv,
        cots,
        rotation,
        envelope.reshape(1, edges),
        src,
        tgt,
        edge_count.reshape(1, 1),
        valid,
    )
    gz, g1, g2 = made[:3]
    own, halo_rows = call(
        back_kernel,
        (sds((rows, atoms), F32), sds((slots, rows), BF)),
        (
            pltpu.VMEM((235, edges), F32),
            pltpu.VMEM((29 * width, edges), F32),
            pltpu.VMEM((rows, edges), BF),
        ),
        flops=10**10,
    )(
        gz,
        g1,
        g2,
        weight_zero.reshape(7 * width, 7 * channels),
        weight_one.reshape(12 * width, 6 * channels),
        weight_two.reshape(10 * width, 5 * channels),
        rotation,
        src,
    )
    back = lax.all_to_all(halo_rows, "atoms", split_axis=0, concat_axis=0, tiled=True)
    grad_x = call(join_kernel, sds((rows, atoms), F32))(own, back, sends)

    dz = made[3][:, : 7 * width].reshape(7, channels, 7, width)
    d1 = made[4].reshape(6, channels, 2, 6, width)
    d2 = made[5][:, : 10 * width].reshape(5, channels, 2, 5, width)
    dz = lax.psum_scatter(dz, "atoms", scatter_dimension=1, tiled=True)
    d1 = lax.psum_scatter(d1, "atoms", scatter_dimension=1, tiled=True)
    d2 = lax.psum_scatter(d2, "atoms", scatter_dimension=1, tiled=True)
    return (
        grad_x.reshape(49, width, atoms),
        dz.transpose(2, 3, 0, 1) * factor,
        d1.transpose(2, 3, 4, 0, 1) * factor,
        d2.transpose(2, 3, 4, 0, 1) * factor,
    )


def solution(mesh):
    in_specs = (
        P(None, "chan", "atoms"),
        P(None, "chan", "atoms"),
        P(None, "atoms"),
        P("atoms"),
        P("atoms"),
        P("atoms"),
        P("atoms"),
        P("atoms", None, None),
        P(None, "atoms"),
        P(None, "chan", None, None),
        P(None, None, "chan", None, None),
        P(None, None, "chan", None, None),
    )
    out_specs = (
        P(None, "chan", "atoms"),
        P(None, "chan", None, "atoms"),
        P(None, None, "chan", None, "atoms"),
        P(None, None, "chan", None, "atoms"),
    )
    return jax.shard_map(
        on_device, mesh=mesh, in_specs=in_specs, out_specs=out_specs, check_vma=False
    )
```
